32 devices in a mesh: tp: 4 (over y, x), grp: 8 (over z, core).
Axes of the slice: x: 2, y: 2, z: 4, core: 2. Of those that a mesh axis runs over, the one named last changes fastest.
Arguments:
- embeds: bfloat16 [2, 32, 8192], P(None, 'grp'), may hold values from -6 to 6
- ssm_state: bfloat16 [2, 32, 128, 64, 128], P(None, 'grp', 'tp'), may hold values from -2 to 2
- conv_state: bfloat16 [2, 32, 3, 8192], P(None, 'grp', None, 'tp'), may hold values from -6 to 6
- norm_gain: float32 [2, 8192], replicated, may hold values from 0.25 to 1.75
- in_weight: bfloat16 [2, 8192, 2, 8192], P(None, 'grp', None, 'tp'), may hold values from -0.0625 to 0.0625
- group_weight: bfloat16 [2, 8192, 384], P(None, 'grp'), may hold values from -0.03125 to 0.03125
- dt_bias: float32 [2, 128], P(None, 'tp'), may hold values from -2 to 1
- a_log: float32 [2, 128], P(None, 'tp'), may hold values from -1.5 to 1.5
- skip_gain: float32 [2, 128], P(None, 'tp'), may hold values from 0.5 to 1.5
- conv_weight: float32 [2, 4, 8192], P(None, None, 'tp'), may hold values from -3 to 3
- conv_bias: float32 [2, 8192], P(None, 'tp'), may hold values from -2 to 2
- out_weight: bfloat16 [2, 8192, 8192], P(None, 'tp', 'grp'), may hold values from -0.0625 to 0.0625
- leave_row: int32 [8], P('grp'), may hold values from 0 to 3
- arrive_from: int32 [8], P('grp'), may hold values from 0 to 7, as said below
Outputs:
- out_hidden: bfloat16 [2, 32, 8192], P(None, 'grp', 'tp')
The draws below stay inside these ranges and needn't reach their ends.
Inputs may be any that keep to these rules, and one draw needn't show every extreme that they name: Every group appears exactly once in arrive_from: each group's leaving row fills exactly one freed slot.
All inputs are finite; a program needn't handle non-finite values.
Results may differ from the reference program's by a relative error of at most 0.02.
Values may be sent and summed in bfloat16 or wider, within the bound.
A program may use at most 128 MiB of HBM per device.

```python
import jax
import jax.numpy as jnp
from jax import lax

D = 8192
HEAD_DIM = 64
CONV = 4
INNER = 8192
STATE = 128
LAYERS = 2
STEPS = 2
ROW_DEV = 4
HEADS = 128
GROUPS = 8
ROWS = 32


def place_value(perm, position, wanted):
    where_now = jnp.argmax(perm == wanted).astype(jnp.int32)
    previous = perm[position]
    perm = perm.at[where_now].set(previous)
    return perm.at[position].set(wanted)


def draw_arrive_from(key, part):
    perm = jax.random.permutation(jax.random.fold_in(key, 11), GROUPS).astype(jnp.int32)
    first = jax.random.randint(jax.random.fold_in(key, 12), (), 0, GROUPS).astype(jnp.int32)
    half_away = ((first + GROUPS // 2) % GROUPS).astype(jnp.int32)
    perm = place_value(perm, first, half_away)
    beside = ((first + 1) % GROUPS).astype(jnp.int32)
    perm = place_value(perm, beside, first)
    return perm.astype(jnp.int32)


def with_ends(entries, key, least, largest):
    spot = [jax.random.randint(jax.random.fold_in(key, axis), (), 0, length) for axis, length in enumerate(entries.shape)]
    longest = entries.shape.index(max(entries.shape))
    neighbour = spot[:longest] + [(spot[longest] + 1) % entries.shape[longest]] + spot[longest + 1:]
    return entries.at[tuple(spot)].set(least).at[tuple(neighbour)].set(largest)


def block_scale(key, extent, cuts, smallest, top_value):
    def one(dim, shards_of):
        steps = jax.random.uniform(jax.random.fold_in(jax.random.fold_in(key, 6), dim), (shards_of,), jnp.float32, smallest / len(cuts), top_value / len(cuts))
        return jnp.repeat(jnp.exp(steps), extent[dim] // shards_of).reshape((-1,) + (1,) * (len(extent) - dim - 1))

    level = one(*cuts[0])
    for cut in cuts[1:]:
        level = level * one(*cut)
    return level


def normal_values(stream_key, dims, scale, reach, pieces=(), held_as=jnp.bfloat16):
    array = jax.random.normal(stream_key, dims, jnp.float32) * scale
    if len(pieces) > 0:
        array = block_scale(stream_key, dims, pieces, -0.22, 0.18) * array
    return jnp.clip(array, min=-reach, max=reach).astype(held_as)


def setup_inputs(seed: int = 0) -> dict:
    arg_keys = jax.random.split(jax.random.key(seed), 15)
    embeds = normal_values(arg_keys[0], (STEPS, ROWS, D), 1.0, 6.0, ((1, 8),))
    ssm_state = normal_values(arg_keys[1], (LAYERS, ROWS, HEADS, HEAD_DIM, STATE), 0.3, 2.0, ((1, 8), (2, 4)))
    conv_state = normal_values(arg_keys[2], (LAYERS, ROWS, CONV - 1, INNER), 1.0, 6.0, ((1, 8), (3, 4)))
    norm_gain = jnp.clip(1.0 + 0.15 * jax.random.normal(arg_keys[3], (LAYERS, D), jnp.float32), 0.25, 1.75)
    in_weight = normal_values(arg_keys[4], (LAYERS, D, 2, INNER), D ** -0.5, 0.0625, ((1, 8), (3, 4)))
    group_weight = normal_values(arg_keys[5], (LAYERS, D, 2 * STATE + HEADS), (4 * D) ** -0.5, 0.03125, ((1, 8),))
    dt_bias = jnp.clip(-2.0 + 3.0 * jax.random.uniform(arg_keys[6], (LAYERS, HEADS), jnp.float32) ** block_scale(arg_keys[6], (LAYERS, HEADS), ((1, 4),), -0.2, 0.2), -2.0, 1.0)
    a_log = jnp.clip(jax.random.uniform(arg_keys[7], (LAYERS, HEADS), jnp.float32, -1.5, 1.5) * block_scale(arg_keys[7], (LAYERS, HEADS), ((1, 4),), -0.4, 0.0), -1.5, 1.5)
    skip_gain = jnp.clip(0.5 + 1.0 * jax.random.uniform(arg_keys[8], (LAYERS, HEADS), jnp.float32) ** block_scale(arg_keys[8], (LAYERS, HEADS), ((1, 4),), -0.2, 0.2), 0.5, 1.5)
    conv_weight = normal_values(arg_keys[9], (LAYERS, CONV, INNER), 0.5, 3.0, ((2, 4),), jnp.float32)
    conv_bias = normal_values(arg_keys[10], (LAYERS, INNER), 0.3, 2.0, ((1, 4),), jnp.float32)
    out_weight = normal_values(arg_keys[11], (LAYERS, INNER, D), INNER ** -0.5, 0.0625, ((1, 4), (2, 8)))
    leave_row = with_ends(jax.random.randint(arg_keys[12], (GROUPS,), 0, ROW_DEV), jax.random.fold_in(arg_keys[12], 1), 0, ROW_DEV - 1).astype(jnp.int32)
    arrive_from = draw_arrive_from(jax.random.fold_in(arg_keys[14], 71), 0)
    return {"embeds": embeds, "ssm_state": ssm_state, "conv_state": conv_state, "norm_gain": norm_gain, "in_weight": in_weight, "group_weight": group_weight, "dt_bias": dt_bias, "a_log": a_log, "skip_gain": skip_gain, "conv_weight": conv_weight, "conv_bias": conv_bias, "out_weight": out_weight, "leave_row": leave_row, "arrive_from": arrive_from}


def mamba_layer(hidden, state, conv, gain, w_in, w_group, bias_dt, log_rate, skip, taps, conv_off, w_out):
    rows = hidden.shape[0]
    hf = hidden.astype(jnp.float32)
    normed = (hf * lax.rsqrt(lax.optimization_barrier(jnp.mean(hf * hf, axis=-1, keepdims=True)) + 1e-05) * gain).astype(jnp.bfloat16)
    proj = jnp.dot(normed, w_in.reshape(D, 2 * INNER), preferred_element_type=jnp.float32)
    x_part = proj[:, :INNER].astype(jnp.bfloat16)
    z_part = proj[:, INNER:]
    mix = jnp.dot(normed, w_group, preferred_element_type=jnp.float32)
    b_mat = mix[:, :STATE]
    c_mat = mix[:, STATE:2 * STATE]
    dt_raw = mix[:, 2 * STATE:]
    conv_sum = x_part.astype(jnp.float32) * taps[CONV - 1] + conv_off
    for k in range(CONV - 1):
        conv_sum = conv_sum + conv[:, k].astype(jnp.float32) * taps[k]
    xc = jax.nn.silu(conv_sum)
    new_conv = jnp.concatenate([conv[:, 1:], x_part[:, None, :]], axis=1)
    step_size = jax.nn.softplus(dt_raw + bias_dt)
    decay = jnp.exp(-step_size * jnp.exp(log_rate))
    xh = xc.reshape(rows, HEADS, HEAD_DIM)
    fresh = state.astype(jnp.float32) * decay[:, :, None, None] + (step_size[:, :, None] * xh)[..., None] * b_mat[:, None, None, :]
    out_y = lax.optimization_barrier(jnp.sum(fresh * c_mat[:, None, None, :], axis=-1)) + skip[None, :, None] * xh
    gated = (out_y.reshape(rows, INNER) * jax.nn.silu(z_part)).astype(jnp.bfloat16)
    delta = jnp.dot(gated, w_out, preferred_element_type=jnp.float32).astype(jnp.bfloat16)
    hidden = (hf + delta.astype(jnp.float32)).astype(jnp.bfloat16)
    return (hidden, fresh.astype(jnp.bfloat16), new_conv)

def reference(embeds, ssm_state, conv_state, norm_gain, in_weight, group_weight, dt_bias, a_log, skip_gain, conv_weight, conv_bias, out_weight, leave_row, arrive_from):
    states = [ssm_state[i] for i in range(LAYERS)]
    convs = [conv_state[i] for i in range(LAYERS)]
    groups_idx = jnp.arange(GROUPS, dtype=jnp.int32)
    target = (groups_idx * ROW_DEV + leave_row).astype(jnp.int32)
    source = (arrive_from * ROW_DEV + leave_row[arrive_from]).astype(jnp.int32)
    results = []
    for section in range(STEPS):
        if section > 0:
            for i in range(LAYERS):
                states[i] = states[i].at[target].set(states[i][source])
                convs[i] = convs[i].at[target].set(convs[i][source])
        hidden = embeds[section]
        for i in range(LAYERS):
            hidden, states[i], convs[i] = mamba_layer(hidden, states[i], convs[i], norm_gain[i], in_weight[i], group_weight[i], dt_bias[i], a_log[i], skip_gain[i], conv_weight[i], conv_bias[i], out_weight[i])
        results.append(hidden)
    return jnp.stack(results)
```

```python
import functools

import jax
import jax.numpy as jnp
from jax import lax
from jax.experimental import pallas as pl
from jax.experimental.pallas import tpu as pltpu
from jax.sharding import PartitionSpec as P

F32 = jnp.float32
BF = jnp.bfloat16
LANES = 128


def iota(shape, dim):
    return lax.broadcasted_iota(jnp.int32, shape, dim)


def mm(a, b):
    return jnp.dot(a, b, preferred_element_type=F32)


def silu(v):
    return v / (1.0 + jnp.exp(-v))


def one_hot(cond):
    return cond.astype(F32).astype(BF)


def remote(src, dst, send_sem, recv_sem, device):
    return pltpu.make_async_remote_copy(
        src_ref=src,
        dst_ref=dst,
        send_sem=send_sem,
        recv_sem=recv_sem,
        device_id=device,
        device_id_type=pl.DeviceIdType.MESH,
    )


def exact_mm(values, hot):
    rest = values
    total = jnp.zeros((values.shape[0], hot.shape[1]), F32)
    for _ in range(3):
        piece = rest.astype(BF)
        rest = rest - piece.astype(F32)
        total = total + mm(piece, hot)
    return total


def kernel(
    groups, parts, heads_dev, head_dim, chunk_in, chunk_out,
    emb, conv, gain, dt_bias, a_log, skip, taps, cbias, leave, arrive, state, w_in, w_grp, w_out,
    out,
    win_v, wg_v, wout_v, st_v,
    conv_v, gain_v, bias_v, rate_v, skip_v, taps_v, cbias_v, who,
    emb_r, info, info_r, e32, info32, pre, sel, lhs, hxs,
    m_send, m_pair, m_z, m_recv, a_send, a_pair, a_z, a_recv,
    b_send, b_recv, c_send, c_recv, h_send, h_recv, p_send, p_recv, gat,
    load_sem, in_sem, small_sem, own_sem, es_sem, er_sem, is_sem, ir_sem, mps_sem, mpr_sem, ms_sem, mr_sem,
    aps_sem, apr_sem, as_sem, ar_sem,
    bs_sem, br_sem, cs_sem, cr_sem, hs_sem, hr_sem, ps_sem, pr_sem,
):
    g = lax.axis_index("grp")
    t = lax.axis_index("tp")
    steps, row_dev, width = emb.shape
    layers = gain.shape[0]
    block = width // groups
    both = steps * row_dev
    rows = groups * both
    channels = taps.shape[2]
    taps_count = taps.shape[1]
    state_dim = st_v.shape[3]
    mix_width = wg_v.shape[2]
    n_in = channels // chunk_in
    n_out = block // chunk_out
    share = groups // parts
    half = groups // 2
    core = lax.rem(g, 2)
    chip = g // 2
    partner = g + 1 - 2 * core
    owner = g // share
    n_tiles = channels // LANES
    tiles_in = chunk_in // LANES

    barrier = pltpu.get_barrier_semaphore()
    for d in range(1, groups):
        pl.semaphore_signal(
            barrier, inc=1, device_id={"grp": lax.rem(g + d, groups)},
            device_id_type=pl.DeviceIdType.MESH,
        )
    for d in range(1, parts):
        pl.semaphore_signal(
            barrier, inc=1, device_id={"tp": lax.rem(t + d, parts)},
            device_id_type=pl.DeviceIdType.MESH,
        )

    def columns(who_):
        return pl.ds(pl.multiple_of(who_ * block, block), block)

    loads = {}

    def load(name, src, dst, sem):
        loads[name] = pltpu.make_async_copy(src, dst, sem)
        loads[name].start()

    load("leave", leave, who.at[0], small_sem.at[0])
    load("arrive", arrive, who.at[1], small_sem.at[1])
    load("emb", emb.at[:, :, columns(g)], emb_r.at[g], own_sem)
    load("gain", gain.at[:, columns(g)], gain_v, small_sem.at[2])
    load("bias", dt_bias, bias_v, small_sem.at[3])
    load("rate", a_log, rate_v, small_sem.at[4])
    load("skip", skip, skip_v, small_sem.at[5])
    load("taps", taps, taps_v, small_sem.at[6])
    load("cbias", cbias, cbias_v, small_sem.at[7])
    load("conv", conv, conv_v, small_sem.at[8])

    def load_in(l):
        load((l, "grp"), w_grp.at[l], wg_v.at[l], load_sem.at[l, 0])
        for n in range(n_tiles):
            tile = slice(n * LANES, (n + 1) * LANES)
            load((l, n), w_in.at[l, :, :, tile], win_v.at[l, n], in_sem.at[l, n])

    def load_rest(l):
        load((l, "state"), state.at[l], st_v.at[l], load_sem.at[l, 1])
        load((l, "out"), w_out.at[l], wout_v.at[l], load_sem.at[l, 2])

    load_in(0)
    loads["leave"].wait()
    loads["arrive"].wait()
    first_half = iota((both, LANES), 1) < LANES // 2
    info[...] = jnp.where(first_half, who[0, 0].astype(F32), who[1, 0].astype(F32))

    pl.semaphore_wait(barrier, groups - 1 + parts - 1)

    first_sends = []
    for d in range(1, groups):
        peer = lax.rem(g + d, groups)
        cp = remote(emb.at[:, :, columns(peer)], emb_r.at[g], es_sem.at[d], er_sem.at[g], {"grp": peer})
        cp.start()
        first_sends.append(cp)
        cp = remote(info, info_r.at[g], is_sem.at[d], ir_sem.at[g], {"grp": peer})
        cp.start()
        first_sends.append(cp)
    info_r[g] = info[...]
    load_rest(0)
    for l in range(1, layers):
        load_in(l)
        load_rest(l)

    n_heads = sel.shape[0]
    sel[...] = one_hot(
        iota((n_heads, channels), 0) == t * heads_dev + iota((n_heads, channels), 1) // head_dim
    )
    own_head = one_hot(iota((heads_dev, channels), 1) // head_dim == iota((heads_dev, channels), 0))
    place = one_hot(iota((heads_dev, n_heads), 1) == t * heads_dev + iota((heads_dev, n_heads), 0))
    spread = one_hot(iota((LANES, 2 * LANES), 1) // 2 == iota((LANES, 2 * LANES), 0))
    even = lax.rem(iota((rows, 2 * LANES), 1), 2) == 0
    for name in ("bias", "rate", "skip", "cbias", "conv", "taps"):
        loads[name].wait()
    bias_all = exact_mm(bias_v[...], place)
    rate_all = exact_mm(jnp.exp(rate_v[...]), place)
    skip_all = exact_mm(skip_v[...], own_head)
    for l in range(layers):
        for s in range(steps):
            total = jnp.zeros((row_dev, channels), F32)
            for k in range(taps_count - 1):
                if s + k <= taps_count - 2:
                    total = total + conv_v[l, s + k].astype(F32) * taps_v[l, k : k + 1, :]
            pre[l, s * row_dev : (s + 1) * row_dev, :] = total + cbias_v[l : l + 1, :]

    loads["gain"].wait()
    loads["emb"].wait()
    for d in range(1, groups):
        src = lax.rem(g + groups - d, groups)
        remote(emb.at[:, :, columns(src)], emb_r.at[src], es_sem.at[d], er_sem.at[src], {"grp": src}).wait_recv()
        remote(info, info_r.at[src], is_sem.at[d], ir_sem.at[src], {"grp": src}).wait_recv()
    for i in range(groups):
        for s in range(steps):
            e32[i * both + s * row_dev : i * both + (s + 1) * row_dev, :] = emb_r[i, s].astype(F32)
        info32[i * both : (i + 1) * both, :] = info_r[i]

    square_shape = (rows, rows)
    row_i = iota(square_shape, 0)
    col_i = iota(square_shape, 1)
    on_diag = row_i == col_i
    leave_of_row = jnp.broadcast_to(info32[:, 0:1], square_shape)
    from_of_row = jnp.broadcast_to(info32[:, LANES // 2 : LANES // 2 + 1], square_shape)
    leave_of_col = jnp.sum(jnp.where(on_diag, leave_of_row, 0.0), axis=0, keepdims=True)
    from_of_col = jnp.sum(jnp.where(on_diag, from_of_row, 0.0), axis=0, keepdims=True)
    slot_row = lax.rem(row_i, row_dev).astype(F32)
    slot_col = lax.rem(col_i, row_dev).astype(F32)
    step_row = lax.rem(row_i // row_dev, steps)
    step_col = lax.rem(col_i // row_dev, steps)
    group_row = (row_i // both).astype(F32)
    group_col = (col_i // both).astype(F32)
    diag = jnp.where(on_diag, 1.0, 0.0)
    same_step = jnp.where(step_row == step_col, 1.0, 0.0)
    hit = jnp.where(group_col == from_of_row, same_step, 0.0) * jnp.where(slot_col == leave_of_col, 1.0, 0.0)
    moved_row = jnp.where(slot_row == leave_of_row, hit, diag)
    hit_t = jnp.where(group_row == from_of_col, same_step, 0.0) * jnp.where(slot_row == leave_of_row, 1.0, 0.0)
    moved_col = jnp.where(slot_col == leave_of_col, hit_t, diag)
    to_slot = [jnp.where(step_row >= n, moved_row, diag).astype(BF) for n in range(1, steps)]
    to_home = [jnp.where(step_col >= n, moved_col, diag).astype(BF) for n in range(1, steps)]

    start = e32[...]
    for hop in to_home:
        start = mm(hop, start.astype(BF))
    hxs[...] = start

    sends = first_sends
    row_step = iota((both, chunk_in), 0) // row_dev
    slot16 = lax.rem(iota((2 * both, channels), 0), row_dev)

    def repeat_step(v, e):
        return jnp.concatenate([v[e * row_dev : (e + 1) * row_dev]] * steps, axis=0)

    for l in range(layers):
        last = l == layers - 1
        done = sends
        sends = []
        hx = hxs[...]
        gained = (hx * gain_v[l : l + 1, :]).astype(BF)
        loads[l, "grp"].wait()
        mix = mm(gained, wg_v[l])
        square = jnp.broadcast_to(jnp.sum(hx * hx, axis=1, keepdims=True), (rows, LANES))
        for i in range(groups):
            m_send[l, i % 2, i // 2, :, :mix_width] = mix[i * both : (i + 1) * both]
            m_send[l, i % 2, i // 2, :, mix_width:] = square[i * both : (i + 1) * both]
        m_cross = remote(m_send.at[l, 1 - core], m_pair.at[l], mps_sem.at[l], mpr_sem.at[l], {"grp": partner})
        m_cross.start()
        sends.append(m_cross)
        for j in range(block // LANES):
            wide = mm(gained[:, j * LANES : (j + 1) * LANES], spread)
            lhs[0:rows, 2 * j * LANES : 2 * (j + 1) * LANES] = jnp.where(even, wide, 0.0).astype(BF)
            lhs[rows : 2 * rows, 2 * j * LANES : 2 * (j + 1) * LANES] = jnp.where(even, 0.0, wide).astype(BF)
        crossing = []
        for c in range(n_in + 1):
            if c < n_in:
                tiles = []
                for n in range(c * tiles_in, (c + 1) * tiles_in):
                    loads[l, n].wait()
                    tiles.append(win_v[l, n].reshape(2 * block, LANES))
                acc = mm(lhs[...], jnp.concatenate(tiles, axis=1))
                for i in range(groups):
                    a_send[l, c, i % 2, i // 2] = jnp.concatenate(
                        [acc[i * both : (i + 1) * both], acc[rows + i * both : rows + (i + 1) * both]], axis=0
                    ).astype(BF)
                cross = remote(
                    a_send.at[l, c, 1 - core], a_pair.at[l, c], aps_sem.at[l, c], apr_sem.at[l, c], {"grp": partner}
                )
                cross.start()
                sends.append(cross)
                crossing.append(cross)
            if c == 0:
                m_cross.wait_recv()
                m_z[l] = m_send[l, core] + m_pair[l]
                for d in range(1, half):
                    to = lax.rem(chip + d, half)
                    cp = remote(
                        m_z.at[l, to], m_recv.at[l, chip], ms_sem.at[l, d], mr_sem.at[l, chip],
                        {"grp": 2 * to + core},
                    )
                    cp.start()
                    sends.append(cp)
                m_recv[l, chip] = m_z[l, chip]
            else:
                e = c - 1
                crossing[e].wait_recv()
                a_z[l, e] = (a_send[l, e, core].astype(F32) + a_pair[l, e].astype(F32)).astype(BF)
                for d in range(1, half):
                    to = lax.rem(chip + d, half)
                    cp = remote(
                        a_z.at[l, e, to], a_recv.at[l, e, chip], as_sem.at[l, e, d], ar_sem.at[l, e, chip],
                        {"grp": 2 * to + core},
                    )
                    cp.start()
                    sends.append(cp)
                a_recv[l, e, chip] = a_z[l, e, chip]

        if last:
            final = hx.astype(BF)
            for hop in to_slot:
                final = mm(hop, final).astype(BF)
            final = final.astype(F32)
            for i in range(groups):
                h_send[i] = final[i * both : (i + 1) * both].astype(BF)

            @pl.when(owner == t)
            def _():
                for d in range(1, groups):
                    peer = lax.rem(g + d, groups)
                    remote(
                        h_send.at[peer], h_recv.at[lax.rem(g, share)], hs_sem.at[d],
                        hr_sem.at[lax.rem(g, share)], {"grp": peer},
                    ).start()
                h_recv[lax.rem(g, share)] = h_send[g]

        for cp in done:
            cp.wait_send()
        for d in range(1, half):
            src = lax.rem(chip + half - d, half)
            remote(
                m_z.at[l, src], m_recv.at[l, src], ms_sem.at[l, d], mr_sem.at[l, src], {"grp": 2 * src + core}
            ).wait_recv()
        msum = m_recv[l, 0]
        for i in range(1, half):
            msum = msum + m_recv[l, i]
        scale = lax.rsqrt(msum[:, mix_width : mix_width + 1] / width + 1e-05)
        b_mat = msum[:, :state_dim] * scale
        c_mat = msum[:, state_dim : 2 * state_dim] * scale
        pre_dt = msum[:, 2 * state_dim : mix_width] * scale + bias_all[l : l + 1, :]
        step_size = jnp.maximum(pre_dt, 0.0) + jnp.log1p(jnp.exp(-jnp.abs(pre_dt)))
        decay = jnp.exp(-step_size * rate_all[l : l + 1, :])
        pieces = []
        for v in (step_size, decay):
            hi = v.astype(BF).astype(F32)
            pieces += [hi, v - hi]
        wide = mm(jnp.concatenate(pieces, axis=0).astype(BF), sel[...])
        step_ch = wide[0:both] + wide[both : 2 * both]
        decay_ch = wide[2 * both : 3 * both] + wide[3 * both : 4 * both]
        bc = [jnp.sum(repeat_step(b_mat, e) * c_mat, axis=1, keepdims=True) for e in range(steps)]
        c_hi = c_mat.astype(BF).astype(F32)
        c_both = jnp.concatenate([c_hi, c_mat - c_hi], axis=0).astype(BF)
        loads[l, "state"].wait()
        total = jnp.zeros((2 * both, channels), F32)
        for r in range(row_dev):
            got = lax.dot_general(
                c_both, st_v[l, r], (((1,), (1,)), ((), ())), preferred_element_type=F32
            )
            total = jnp.where(slot16 == r, got, total)
        state_y = total[0:both] + total[both : 2 * both]

        for c in range(n_in):
            cols = slice(c * chunk_in, (c + 1) * chunk_in)
            for d in range(1, half):
                src = lax.rem(chip + half - d, half)
                remote(
                    a_z.at[l, c, src], a_recv.at[l, c, src], as_sem.at[l, c, d], ar_sem.at[l, c, src],
                    {"grp": 2 * src + core},
                ).wait_recv()
            asum = a_recv[l, c, 0].astype(F32)
            for i in range(1, half):
                asum = asum + a_recv[l, c, i].astype(F32)
            x = (asum[0:both] * scale).astype(BF).astype(F32)
            z = asum[both : 2 * both] * scale
            conv_sum = pre[l, :, cols] + x * taps_v[l, taps_count - 1 : taps_count, cols]
            for e in range(1, steps):
                tap = taps_count - 1 - e
                if tap >= 0:
                    before = jnp.concatenate(
                        [jnp.zeros((e * row_dev, chunk_in), F32), x[: both - e * row_dev]], axis=0
                    )
                    conv_sum = conv_sum + before * taps_v[l, tap : tap + 1, cols]
            xc = silu(conv_sum)
            dtx = step_ch[:, cols] * xc
            dec = decay_ch[:, cols]
            acc_y = state_y[:, cols]
            for e in range(steps):
                later = repeat_step(dec, e) * acc_y + repeat_step(dtx, e) * bc[e]
                acc_y = later if e == 0 else jnp.where(row_step >= e, later, acc_y)
            gated = ((acc_y + skip_all[l : l + 1, cols] * xc) * silu(z)).astype(BF)
            b_send[l, c] = gated
            b_recv[l, c, g] = gated
            for d in range(1, groups):
                peer = lax.rem(g + d, groups)
                cp = remote(
                    b_send.at[l, c], b_recv.at[l, c, g], bs_sem.at[l, c, d], br_sem.at[l, c, g], {"grp": peer}
                )
                cp.start()
                sends.append(cp)

        loads[l, "out"].wait()
        gated_all = []
        for c in range(n_in):
            for d in range(1, groups):
                src = lax.rem(g + groups - d, groups)
                remote(
                    b_send.at[l, c], b_recv.at[l, c, src], bs_sem.at[l, c, d], br_sem.at[l, c, src], {"grp": src}
                ).wait_recv()
            for i in range(groups):
                gat[c, i * both : (i + 1) * both, :] = b_recv[l, c, i].astype(F32)
            part = gat[c].astype(BF)
            if last:
                for hop in to_slot:
                    part = mm(hop, part).astype(BF)
            gated_all.append(part)
        gated_all = jnp.concatenate(gated_all, axis=1)

        for n in range(n_out):
            cols = slice(n * chunk_out, (n + 1) * chunk_out)
            part = mm(gated_all, wout_v[l, :, cols])
            if not last:
                c_send[l, n] = part.astype(BF)
                c_recv[l, n, t] = c_send[l, n]
                for d in range(1, parts):
                    peer = lax.rem(t + d, parts)
                    cp = remote(
                        c_send.at[l, n], c_recv.at[l, n, t], cs_sem.at[l, n, d], cr_sem.at[l, n, t], {"tp": peer}
                    )
                    cp.start()
                    sends.append(cp)
            else:
                spot = lax.rem(g, share)
                for i in range(groups):
                    p_send[n, i] = part[i * both : (i + 1) * both].astype(BF)
                for d in range(1, groups):
                    peer = lax.rem(g + d, groups)
                    cp = remote(
                        p_send.at[n, peer], p_recv.at[n, spot, t], ps_sem.at[n, d], pr_sem.at[n, spot, t],
                        {"grp": peer, "tp": owner},
                    )
                    cp.start()
                    sends.append(cp)

                @pl.when(owner == t)
                def _(n=n):
                    p_recv[n, spot, t] = p_send[n, g]

                @pl.when(owner != t)
                def _(n=n):
                    remote(
                        p_send.at[n, g], p_recv.at[n, spot, t], ps_sem.at[n, 0], pr_sem.at[n, spot, t],
                        {"grp": g, "tp": owner},
                    ).start()

        if not last:
            for n in range(n_out):
                for d in range(1, parts):
                    src = lax.rem(t + parts - d, parts)
                    remote(
                        c_send.at[l, n], c_recv.at[l, n, src], cs_sem.at[l, n, d], cr_sem.at[l, n, src], {"tp": src}
                    ).wait_recv()
                dsum = c_recv[l, n, 0].astype(F32)
                for i in range(1, parts):
                    dsum = dsum + c_recv[l, n, i].astype(F32)
                cols = slice(n * chunk_out, (n + 1) * chunk_out)
                hxs[:, cols] = (hxs[:, cols] + dsum.astype(BF).astype(F32)).astype(BF).astype(F32)

    for cp in sends:
        cp.wait_send()

    @pl.when(owner == t)
    def _():
        for d in range(1, groups):
            peer = lax.rem(g + d, groups)
            remote(
                h_send.at[peer], h_recv.at[lax.rem(g, share)], hs_sem.at[d],
                hr_sem.at[lax.rem(g, share)], {"grp": peer},
            ).wait_send()

    @pl.when(owner != t)
    def _():
        for n in range(n_out):
            remote(
                p_send.at[n, g], p_recv.at[n, lax.rem(g, share), t], ps_sem.at[n, 0],
                pr_sem.at[n, lax.rem(g, share), t], {"grp": g, "tp": owner},
            ).wait_send()

    for j in range(share):
        src = t * share + j

        @pl.when(src != g)
        def _(j=j, src=src):
            remote(h_send.at[src], h_recv.at[j], hs_sem.at[1], hr_sem.at[j], {"grp": src}).wait_recv()

    for n in range(n_out):
        for j in range(share):
            src = t * share + j
            for i in range(parts):

                @pl.when((src != g) | (t != i))
                def _(n=n, j=j, i=i, src=src):
                    remote(
                        p_send.at[n, 0], p_recv.at[n, j, i], ps_sem.at[n, 1], pr_sem.at[n, j, i],
                        {"grp": src, "tp": i},
                    ).wait_recv()

            dsum = p_recv[n, j, 0].astype(F32)
            for i in range(1, parts):
                dsum = dsum + p_recv[n, j, i].astype(F32)
            cols = slice(n * chunk_out, (n + 1) * chunk_out)
            result = h_recv[j, :, cols].astype(F32) + dsum.astype(BF).astype(F32)
            for s in range(steps):
                out[s, :, j * block + n * chunk_out : j * block + (n + 1) * chunk_out] = result[
                    s * row_dev : (s + 1) * row_dev
                ].astype(BF)


def local(
    embeds, ssm_state, conv_state, norm_gain, in_weight, group_weight, dt_bias, a_log,
    skip_gain, conv_weight, conv_bias, out_weight, leave_row, arrive_from,
):
    groups = lax.axis_size("grp")
    parts = lax.axis_size("tp")
    steps, row_dev, width = embeds.shape
    layers, _, heads_dev, head_dim, state_dim = ssm_state.shape
    block = in_weight.shape[1]
    channels = in_weight.shape[3]
    mix_width = group_weight.shape[2]
    n_heads = mix_width - 2 * state_dim
    taps_count = conv_weight.shape[1]
    both = steps * row_dev
    rows = groups * both
    share = groups // parts
    half = groups // 2
    chunk_in = min(512, channels)
    chunk_out = min(512, block)
    n_in = channels // chunk_in
    n_out = block // chunk_out

    state = ssm_state.reshape(layers, row_dev, channels, state_dim)
    conv = conv_state.transpose(0, 2, 1, 3)
    vm = pl.BlockSpec(memory_space=pltpu.VMEM)
    anywhere = pl.BlockSpec(memory_space=pl.ANY)
    dma = pltpu.SemaphoreType.DMA
    V = pltpu.VMEM
    return pl.pallas_call(
        functools.partial(kernel, groups, parts, heads_dev, head_dim, chunk_in, chunk_out),
        out_shape=jax.ShapeDtypeStruct((steps, row_dev, width // parts), BF),
        in_specs=[anywhere] * 14,
        out_specs=vm,
        scratch_shapes=[
            V((layers, channels // LANES, block, 2, LANES), BF),
            V((layers, block, mix_width), BF),
            V((layers, channels, block), BF),
            V((layers, row_dev, channels, state_dim), BF),
            V((layers, taps_count - 1, row_dev, channels), BF),
            V((layers, block), F32),
            V((layers, heads_dev), F32),
            V((layers, heads_dev), F32),
            V((layers, heads_dev), F32),
            V((layers, taps_count, channels), F32),
            V((layers, channels), F32),
            pltpu.SMEM((2, 1), jnp.int32),
            V((groups, steps, row_dev, block), BF),
            V((both, LANES), F32),
            V((groups, both, LANES), F32),
            V((rows, block), F32),
            V((rows, LANES), F32),
            V((layers, both, channels), F32),
            V((n_heads, channels), BF),
            V((2 * rows, 2 * block), BF),
            V((rows, block), F32),
            V((layers, 2, half, both, mix_width + LANES), F32),
            V((layers, half, both, mix_width + LANES), F32),
            V((layers, half, both, mix_width + LANES), F32),
            V((layers, half, both, mix_width + LANES), F32),
            V((layers, n_in, 2, half, 2 * both, chunk_in), BF),
            V((layers, n_in, half, 2 * both, chunk_in), BF),
            V((layers, n_in, half, 2 * both, chunk_in), BF),
            V((layers, n_in, half, 2 * both, chunk_in), BF),
            V((layers, n_in, both, chunk_in), BF),
            V((layers, n_in, groups, both, chunk_in), BF),
            V((layers, n_out, rows, chunk_out), BF),
            V((layers, n_out, parts, rows, chunk_out), BF),
            V((groups, both, block), BF),
            V((share, both, block), BF),
            V((n_out, groups, both, chunk_out), BF),
            V((n_out, share, parts, both, chunk_out), BF),
            V((n_in, rows, chunk_in), F32),
            dma((layers, 3)),
            dma((layers, channels // LANES)),
            dma((9,)),
            dma,
            dma((groups,)),
            dma((groups,)),
            dma((groups,)),
            dma((groups,)),
            dma((layers,)),
            dma((layers,)),
            dma((layers, half)),
            dma((layers, half)),
            dma((layers, n_in)),
            dma((layers, n_in)),
            dma((layers, n_in, half)),
            dma((layers, n_in, half)),
            dma((layers, n_in, groups)),
            dma((layers, n_in, groups)),
            dma((layers, n_out, parts)),
            dma((layers, n_out, parts)),
            dma((groups,)),
            dma((share,)),
            dma((n_out, groups)),
            dma((n_out, share, parts)),
        ],
        compiler_params=pltpu.CompilerParams(
            collective_id=0, has_side_effects=True, vmem_limit_bytes=60 * 2**20
        ),
    )(
        embeds, conv, norm_gain, dt_bias, a_log, skip_gain, conv_weight, conv_bias, leave_row, arrive_from,
        state, in_weight, group_weight, out_weight,
    )


def solution(mesh):
    placed = (
        P(None, "grp", None),
        P(None, "grp", "tp", None, None),
        P(None, "grp", None, "tp"),
        P(),
        P(None, "grp", None, "tp"),
        P(None, "grp", None),
        P(None, "tp"),
        P(None, "tp"),
        P(None, "tp"),
        P(None, None, "tp"),
        P(None, "tp"),
        P(None, "tp", "grp"),
        P("grp"),
        P("grp"),
    )
    return jax.shard_map(
        local, mesh=mesh, in_specs=placed, out_specs=P(None, "grp", "tp"), check_vma=False
    )
```

```python
import functools

import jax
import jax.numpy as jnp
from jax import lax
from jax.experimental import pallas as pl
from jax.experimental.pallas import tpu as pltpu
from jax.sharding import PartitionSpec as P

F32 = jnp.float32
BF = jnp.bfloat16
LANES = 128


def iota(shape, dim):
    return lax.broadcasted_iota(jnp.int32, shape, dim)


def mm(a, b):
    return jnp.dot(a, b, preferred_element_type=F32)


def silu(v):
    return v / (1.0 + jnp.exp(-v))


def one_hot(cond):
    return cond.astype(F32).astype(BF)


def remote(src, dst, send_sem, recv_sem, device):
    return pltpu.make_async_remote_copy(
        src_ref=src,
        dst_ref=dst,
        send_sem=send_sem,
        recv_sem=recv_sem,
        device_id=device,
        device_id_type=pl.DeviceIdType.MESH,
    )


def exact_mm(values, hot):
    rest = values
    total = jnp.zeros((values.shape[0], hot.shape[1]), F32)
    for _ in range(3):
        piece = rest.astype(BF)
        rest = rest - piece.astype(F32)
        total = total + mm(piece, hot)
    return total


def kernel(
    groups, parts, heads_dev, head_dim, chunk_in, chunk_out,
    emb, conv, gain, dt_bias, a_log, skip, taps, cbias, leave, arrive, state, w_in, w_grp, w_out,
    out,
    win_v, wg_v, wout_v, st_v,
    conv_v, gain_v, bias_v, rate_v, skip_v, taps_v, cbias_v, who,
    emb_r, info, info_r, e32, info32, pre, sel, lhs, hxs,
    m_send, m_pair, m_z, m_recv, a_send, a_pair, a_z, a_recv,
    b_send, b_recv, c_send, c_recv, h_send, h_recv, p_send, p_recv, gat,
    load_sem, in_sem, small_sem, own_sem, es_sem, er_sem, is_sem, ir_sem, mps_sem, mpr_sem, ms_sem, mr_sem,
    aps_sem, apr_sem, as_sem, ar_sem,
    bs_sem, br_sem, cs_sem, cr_sem, hs_sem, hr_sem, ps_sem, pr_sem,
):
    g = lax.axis_index("grp")
    t = lax.axis_index("tp")
    steps, row_dev, width = emb.shape
    layers = gain.shape[0]
    block = width // groups
    both = steps * row_dev
    rows = groups * both
    channels = taps.shape[2]
    taps_count = taps.shape[1]
    state_dim = st_v.shape[3]
    mix_width = wg_v.shape[2]
    n_in = channels // chunk_in
    n_out = block // chunk_out
    share = groups // parts
    half = groups // 2
    core = lax.rem(g, 2)
    chip = g // 2
    partner = g + 1 - 2 * core
    owner = g // share
    w_pairs = w_in.reshape(layers, 2 * block, channels)

    barrier = pltpu.get_barrier_semaphore()
    for d in range(1, groups):
        pl.semaphore_signal(
            barrier, inc=1, device_id={"grp": lax.rem(g + d, groups)},
            device_id_type=pl.DeviceIdType.MESH,
        )
    for d in range(1, parts):
        pl.semaphore_signal(
            barrier, inc=1, device_id={"tp": lax.rem(t + d, parts)},
            device_id_type=pl.DeviceIdType.MESH,
        )

    def columns(who_):
        return pl.ds(pl.multiple_of(who_ * block, block), block)

    loads = {}

    def load(name, src, dst, sem):
        loads[name] = pltpu.make_async_copy(src, dst, sem)
        loads[name].start()

    load("leave", leave, who.at[0], small_sem.at[0])
    load("arrive", arrive, who.at[1], small_sem.at[1])
    load("emb", emb.at[:, :, columns(g)], emb_r.at[g], own_sem)
    load("gain", gain.at[:, columns(g)], gain_v, small_sem.at[2])
    load("bias", dt_bias, bias_v, small_sem.at[3])
    load("rate", a_log, rate_v, small_sem.at[4])
    load("skip", skip, skip_v, small_sem.at[5])
    load("taps", taps, taps_v, small_sem.at[6])
    load("cbias", cbias, cbias_v, small_sem.at[7])
    load("conv", conv, conv_v, small_sem.at[8])

    def load_in(l):
        load((l, "grp"), w_grp.at[l], wg_v.at[l], load_sem.at[l, 0])
        for c in range(n_in):
            cols = slice(c * chunk_in, (c + 1) * chunk_in)
            load((l, c), w_pairs.at[l, :, cols], win_v.at[l, :, cols], in_sem.at[l, c])

    def load_rest(l):
        load((l, "state"), state.at[l], st_v.at[l], load_sem.at[l, 1])
        load((l, "out"), w_out.at[l], wout_v.at[l], load_sem.at[l, 2])

    load_in(0)
    loads["leave"].wait()
    loads["arrive"].wait()
    first_half = iota((both, LANES), 1) < LANES // 2
    info[...] = jnp.where(first_half, who[0, 0].astype(F32), who[1, 0].astype(F32))

    pl.semaphore_wait(barrier, groups - 1 + parts - 1)

    first_sends = []
    for d in range(1, groups):
        peer = lax.rem(g + d, groups)
        cp = remote(emb.at[:, :, columns(peer)], emb_r.at[g], es_sem.at[d], er_sem.at[g], {"grp": peer})
        cp.start()
        first_sends.append(cp)
        cp = remote(info, info_r.at[g], is_sem.at[d], ir_sem.at[g], {"grp": peer})
        cp.start()
        first_sends.append(cp)
    info_r[g] = info[...]
    load_rest(0)
    for l in range(1, layers):
        load_in(l)
        load_rest(l)

    n_heads = sel.shape[0]
    sel[...] = one_hot(
        iota((n_heads, channels), 0) == t * heads_dev + iota((n_heads, channels), 1) // head_dim
    )
    own_head = one_hot(iota((heads_dev, channels), 1) // head_dim == iota((heads_dev, channels), 0))
    place = one_hot(iota((heads_dev, n_heads), 1) == t * heads_dev + iota((heads_dev, n_heads), 0))
    spread = one_hot(iota((LANES, 2 * LANES), 1) // 2 == iota((LANES, 2 * LANES), 0))
    even = lax.rem(iota((rows, 2 * LANES), 1), 2) == 0
    for name in ("bias", "rate", "skip", "cbias", "conv", "taps"):
        loads[name].wait()
    bias_all = exact_mm(bias_v[...], place)
    rate_all = exact_mm(jnp.exp(rate_v[...]), place)
    skip_all = exact_mm(skip_v[...], own_head)
    for l in range(layers):
        for s in range(steps):
            total = jnp.zeros((row_dev, channels), F32)
            for k in range(taps_count - 1):
                if s + k <= taps_count - 2:
                    total = total + conv_v[l, s + k].astype(F32) * taps_v[l, k : k + 1, :]
            pre[l, s * row_dev : (s + 1) * row_dev, :] = total + cbias_v[l : l + 1, :]

    loads["gain"].wait()
    loads["emb"].wait()
    for d in range(1, groups):
        src = lax.rem(g + groups - d, groups)
        remote(emb.at[:, :, columns(src)], emb_r.at[src], es_sem.at[d], er_sem.at[src], {"grp": src}).wait_recv()
        remote(info, info_r.at[src], is_sem.at[d], ir_sem.at[src], {"grp": src}).wait_recv()
    for i in range(groups):
        for s in range(steps):
            e32[i * both + s * row_dev : i * both + (s + 1) * row_dev, :] = emb_r[i, s].astype(F32)
        info32[i * both : (i + 1) * both, :] = info_r[i]

    square_shape = (rows, rows)
    row_i = iota(square_shape, 0)
    col_i = iota(square_shape, 1)
    on_diag = row_i == col_i
    leave_of_row = jnp.broadcast_to(info32[:, 0:1], square_shape)
    from_of_row = jnp.broadcast_to(info32[:, LANES // 2 : LANES // 2 + 1], square_shape)
    leave_of_col = jnp.sum(jnp.where(on_diag, leave_of_row, 0.0), axis=0, keepdims=True)
    from_of_col = jnp.sum(jnp.where(on_diag, from_of_row, 0.0), axis=0, keepdims=True)
    slot_row = lax.rem(row_i, row_dev).astype(F32)
    slot_col = lax.rem(col_i, row_dev).astype(F32)
    step_row = lax.rem(row_i // row_dev, steps)
    step_col = lax.rem(col_i // row_dev, steps)
    group_row = (row_i // both).astype(F32)
    group_col = (col_i // both).astype(F32)
    diag = jnp.where(on_diag, 1.0, 0.0)
    same_step = jnp.where(step_row == step_col, 1.0, 0.0)
    hit = jnp.where(group_col == from_of_row, same_step, 0.0) * jnp.where(slot_col == leave_of_col, 1.0, 0.0)
    moved_row = jnp.where(slot_row == leave_of_row, hit, diag)
    hit_t = jnp.where(group_row == from_of_col, same_step, 0.0) * jnp.where(slot_row == leave_of_row, 1.0, 0.0)
    moved_col = jnp.where(slot_col == leave_of_col, hit_t, diag)
    to_slot = [jnp.where(step_row >= n, moved_row, diag).astype(BF) for n in range(1, steps)]
    to_home = [jnp.where(step_col >= n, moved_col, diag).astype(BF) for n in range(1, steps)]

    start = e32[...]
    for hop in to_home:
        start = mm(hop, start.astype(BF))
    hxs[...] = start

    sends = first_sends
    row_step = iota((both, chunk_in), 0) // row_dev
    slot16 = lax.rem(iota((2 * both, channels), 0), row_dev)

    def repeat_step(v, e):
        return jnp.concatenate([v[e * row_dev : (e + 1) * row_dev]] * steps, axis=0)

    for l in range(layers):
        last = l == layers - 1
        done = sends
        sends = []
        hx = hxs[...]
        gained = (hx * gain_v[l : l + 1, :]).astype(BF)
        loads[l, "grp"].wait()
        mix = mm(gained, wg_v[l])
        square = jnp.broadcast_to(jnp.sum(hx * hx, axis=1, keepdims=True), (rows, LANES))
        for i in range(groups):
            m_send[l, i % 2, i // 2, :, :mix_width] = mix[i * both : (i + 1) * both]
            m_send[l, i % 2, i // 2, :, mix_width:] = square[i * both : (i + 1) * both]
        m_cross = remote(m_send.at[l, 1 - core], m_pair.at[l], mps_sem.at[l], mpr_sem.at[l], {"grp": partner})
        m_cross.start()
        sends.append(m_cross)
        for j in range(block // LANES):
            wide = mm(gained[:, j * LANES : (j + 1) * LANES], spread)
            lhs[0:rows, 2 * j * LANES : 2 * (j + 1) * LANES] = jnp.where(even, wide, 0.0).astype(BF)
            lhs[rows : 2 * rows, 2 * j * LANES : 2 * (j + 1) * LANES] = jnp.where(even, 0.0, wide).astype(BF)
        crossing = []
        for c in range(n_in + 1):
            if c < n_in:
                loads[l, c].wait()
                acc = mm(lhs[...], win_v[l, :, c * chunk_in : (c + 1) * chunk_in])
                for i in range(groups):
                    a_send[l, c, i % 2, i // 2] = jnp.concatenate(
                        [acc[i * both : (i + 1) * both], acc[rows + i * both : rows + (i + 1) * both]], axis=0
                    ).astype(BF)
                cross = remote(
                    a_send.at[l, c, 1 - core], a_pair.at[l, c], aps_sem.at[l, c], apr_sem.at[l, c], {"grp": partner}
                )
                cross.start()
                sends.append(cross)
                crossing.append(cross)
            if c == 0:
                m_cross.wait_recv()
                m_z[l] = m_send[l, core] + m_pair[l]
                for d in range(1, half):
                    to = lax.rem(chip + d, half)
                    cp = remote(
                        m_z.at[l, to], m_recv.at[l, chip], ms_sem.at[l, d], mr_sem.at[l, chip],
                        {"grp": 2 * to + core},
                    )
                    cp.start()
                    sends.append(cp)
                m_recv[l, chip] = m_z[l, chip]
            else:
                e = c - 1
                crossing[e].wait_recv()
                a_z[l, e] = (a_send[l, e, core].astype(F32) + a_pair[l, e].astype(F32)).astype(BF)
                for d in range(1, half):
                    to = lax.rem(chip + d, half)
                    cp = remote(
                        a_z.at[l, e, to], a_recv.at[l, e, chip], as_sem.at[l, e, d], ar_sem.at[l, e, chip],
                        {"grp": 2 * to + core},
                    )
                    cp.start()
                    sends.append(cp)
                a_recv[l, e, chip] = a_z[l, e, chip]

        if last:
            final = hx.astype(BF)
            for hop in to_slot:
                final = mm(hop, final).astype(BF)
            final = final.astype(F32)
            for i in range(groups):
                h_send[i] = final[i * both : (i + 1) * both].astype(BF)

            @pl.when(owner == t)
            def _():
                for d in range(1, groups):
                    peer = lax.rem(g + d, groups)
                    remote(
                        h_send.at[peer], h_recv.at[lax.rem(g, share)], hs_sem.at[d],
                        hr_sem.at[lax.rem(g, share)], {"grp": peer},
                    ).start()
                h_recv[lax.rem(g, share)] = h_send[g]

        for cp in done:
            cp.wait_send()
        for d in range(1, half):
            src = lax.rem(chip + half - d, half)
            remote(
                m_z.at[l, src], m_recv.at[l, src], ms_sem.at[l, d], mr_sem.at[l, src], {"grp": 2 * src + core}
            ).wait_recv()
        msum = m_recv[l, 0]
        for i in range(1, half):
            msum = msum + m_recv[l, i]
        scale = lax.rsqrt(msum[:, mix_width : mix_width + 1] / width + 1e-05)
        b_mat = msum[:, :state_dim] * scale
        c_mat = msum[:, state_dim : 2 * state_dim] * scale
        pre_dt = msum[:, 2 * state_dim : mix_width] * scale + bias_all[l : l + 1, :]
        step_size = jnp.maximum(pre_dt, 0.0) + jnp.log1p(jnp.exp(-jnp.abs(pre_dt)))
        decay = jnp.exp(-step_size * rate_all[l : l + 1, :])
        pieces = []
        for v in (step_size, decay):
            hi = v.astype(BF).astype(F32)
            pieces += [hi, v - hi]
        wide = mm(jnp.concatenate(pieces, axis=0).astype(BF), sel[...])
        step_ch = wide[0:both] + wide[both : 2 * both]
        decay_ch = wide[2 * both : 3 * both] + wide[3 * both : 4 * both]
        bc = [jnp.sum(repeat_step(b_mat, e) * c_mat, axis=1, keepdims=True) for e in range(steps)]
        c_hi = c_mat.astype(BF).astype(F32)
        c_both = jnp.concatenate([c_hi, c_mat - c_hi], axis=0).astype(BF)
        loads[l, "state"].wait()
        total = jnp.zeros((2 * both, channels), F32)
        for r in range(row_dev):
            got = lax.dot_general(
                c_both, st_v[l, r], (((1,), (1,)), ((), ())), preferred_element_type=F32
            )
            total = jnp.where(slot16 == r, got, total)
        state_y = total[0:both] + total[both : 2 * both]

        for c in range(n_in):
            cols = slice(c * chunk_in, (c + 1) * chunk_in)
            for d in range(1, half):
                src = lax.rem(chip + half - d, half)
                remote(
                    a_z.at[l, c, src], a_recv.at[l, c, src], as_sem.at[l, c, d], ar_sem.at[l, c, src],
                    {"grp": 2 * src + core},
                ).wait_recv()
            asum = a_recv[l, c, 0].astype(F32)
            for i in range(1, half):
                asum = asum + a_recv[l, c, i].astype(F32)
            x = (asum[0:both] * scale).astype(BF).astype(F32)
            z = asum[both : 2 * both] * scale
            conv_sum = pre[l, :, cols] + x * taps_v[l, taps_count - 1 : taps_count, cols]
            for e in range(1, steps):
                tap = taps_count - 1 - e
                if tap >= 0:
                    before = jnp.concatenate(
                        [jnp.zeros((e * row_dev, chunk_in), F32), x[: both - e * row_dev]], axis=0
                    )
                    conv_sum = conv_sum + before * taps_v[l, tap : tap + 1, cols]
            xc = silu(conv_sum)
            dtx = step_ch[:, cols] * xc
            dec = decay_ch[:, cols]
            acc_y = state_y[:, cols]
            for e in range(steps):
                later = repeat_step(dec, e) * acc_y + repeat_step(dtx, e) * bc[e]
                acc_y = later if e == 0 else jnp.where(row_step >= e, later, acc_y)
            gated = ((acc_y + skip_all[l : l + 1, cols] * xc) * silu(z)).astype(BF)
            b_send[l, c] = gated
            b_recv[l, c, g] = gated
            for d in range(1, groups):
                peer = lax.rem(g + d, groups)
                cp = remote(
                    b_send.at[l, c], b_recv.at[l, c, g], bs_sem.at[l, c, d], br_sem.at[l, c, g], {"grp": peer}
                )
                cp.start()
                sends.append(cp)

        loads[l, "out"].wait()
        gated_all = []
        for c in range(n_in):
            for d in range(1, groups):
                src = lax.rem(g + groups - d, groups)
                remote(
                    b_send.at[l, c], b_recv.at[l, c, src], bs_sem.at[l, c, d], br_sem.at[l, c, src], {"grp": src}
                ).wait_recv()
            for i in range(groups):
                gat[c, i * both : (i + 1) * both, :] = b_recv[l, c, i].astype(F32)
            part = gat[c].astype(BF)
            if last:
                for hop in to_slot:
                    part = mm(hop, part).astype(BF)
            gated_all.append(part)
        gated_all = jnp.concatenate(gated_all, axis=1)

        for n in range(n_out):
            cols = slice(n * chunk_out, (n + 1) * chunk_out)
            part = mm(gated_all, wout_v[l, :, cols])
            if not last:
                c_send[l, n] = part.astype(BF)
                c_recv[l, n, t] = c_send[l, n]
                for d in range(1, parts):
                    peer = lax.rem(t + d, parts)
                    cp = remote(
                        c_send.at[l, n], c_recv.at[l, n, t], cs_sem.at[l, n, d], cr_sem.at[l, n, t], {"tp": peer}
                    )
                    cp.start()
                    sends.append(cp)
            else:
                spot = lax.rem(g, share)
                for i in range(groups):
                    p_send[n, i] = part[i * both : (i + 1) * both].astype(BF)
                for d in range(1, groups):
                    peer = lax.rem(g + d, groups)
                    cp = remote(
                        p_send.at[n, peer], p_recv.at[n, spot, t], ps_sem.at[n, d], pr_sem.at[n, spot, t],
                        {"grp": peer, "tp": owner},
                    )
                    cp.start()
                    sends.append(cp)

                @pl.when(owner == t)
                def _(n=n):
                    p_recv[n, spot, t] = p_send[n, g]

                @pl.when(owner != t)
                def _(n=n):
                    remote(
                        p_send.at[n, g], p_recv.at[n, spot, t], ps_sem.at[n, 0], pr_sem.at[n, spot, t],
                        {"grp": g, "tp": owner},
                    ).start()

        if not last:
            for n in range(n_out):
                for d in range(1, parts):
                    src = lax.rem(t + parts - d, parts)
                    remote(
                        c_send.at[l, n], c_recv.at[l, n, src], cs_sem.at[l, n, d], cr_sem.at[l, n, src], {"tp": src}
                    ).wait_recv()
                dsum = c_recv[l, n, 0].astype(F32)
                for i in range(1, parts):
                    dsum = dsum + c_recv[l, n, i].astype(F32)
                cols = slice(n * chunk_out, (n + 1) * chunk_out)
                hxs[:, cols] = (hxs[:, cols] + dsum.astype(BF).astype(F32)).astype(BF).astype(F32)

    for cp in sends:
        cp.wait_send()

    @pl.when(owner == t)
    def _():
        for d in range(1, groups):
            peer = lax.rem(g + d, groups)
            remote(
                h_send.at[peer], h_recv.at[lax.rem(g, share)], hs_sem.at[d],
                hr_sem.at[lax.rem(g, share)], {"grp": peer},
            ).wait_send()

    @pl.when(owner != t)
    def _():
        for n in range(n_out):
            remote(
                p_send.at[n, g], p_recv.at[n, lax.rem(g, share), t], ps_sem.at[n, 0],
                pr_sem.at[n, lax.rem(g, share), t], {"grp": g, "tp": owner},
            ).wait_send()

    for j in range(share):
        src = t * share + j

        @pl.when(src != g)
        def _(j=j, src=src):
            remote(h_send.at[src], h_recv.at[j], hs_sem.at[1], hr_sem.at[j], {"grp": src}).wait_recv()

    for n in range(n_out):
        for j in range(share):
            src = t * share + j
            for i in range(parts):

                @pl.when((src != g) | (t != i))
                def _(n=n, j=j, i=i, src=src):
                    remote(
                        p_send.at[n, 0], p_recv.at[n, j, i], ps_sem.at[n, 1], pr_sem.at[n, j, i],
                        {"grp": src, "tp": i},
                    ).wait_recv()

            dsum = p_recv[n, j, 0].astype(F32)
            for i in range(1, parts):
                dsum = dsum + p_recv[n, j, i].astype(F32)
            cols = slice(n * chunk_out, (n + 1) * chunk_out)
            result = h_recv[j, :, cols].astype(F32) + dsum.astype(BF).astype(F32)
            for s in range(steps):
                out[s, :, j * block + n * chunk_out : j * block + (n + 1) * chunk_out] = result[
                    s * row_dev : (s + 1) * row_dev
                ].astype(BF)


def local(
    embeds, ssm_state, conv_state, norm_gain, in_weight, group_weight, dt_bias, a_log,
    skip_gain, conv_weight, conv_bias, out_weight, leave_row, arrive_from,
):
    groups = lax.axis_size("grp")
    parts = lax.axis_size("tp")
    steps, row_dev, width = embeds.shape
    layers, _, heads_dev, head_dim, state_dim = ssm_state.shape
    block = in_weight.shape[1]
    channels = in_weight.shape[3]
    mix_width = group_weight.shape[2]
    n_heads = mix_width - 2 * state_dim
    taps_count = conv_weight.shape[1]
    both = steps * row_dev
    rows = groups * both
    share = groups // parts
    half = groups // 2
    chunk_in = min(512, channels)
    chunk_out = min(512, block)
    n_in = channels // chunk_in
    n_out = block // chunk_out

    state = ssm_state.reshape(layers, row_dev, channels, state_dim)
    conv = conv_state.transpose(0, 2, 1, 3)
    vm = pl.BlockSpec(memory_space=pltpu.VMEM)
    anywhere = pl.BlockSpec(memory_space=pl.ANY)
    dma = pltpu.SemaphoreType.DMA
    V = pltpu.VMEM
    return pl.pallas_call(
        functools.partial(kernel, groups, parts, heads_dev, head_dim, chunk_in, chunk_out),
        out_shape=jax.ShapeDtypeStruct((steps, row_dev, width // parts), BF),
        in_specs=[anywhere] * 14,
        out_specs=vm,
        scratch_shapes=[
            V((layers, 2 * block, channels), BF),
            V((layers, block, mix_width), BF),
            V((layers, channels, block), BF),
            V((layers, row_dev, channels, state_dim), BF),
            V((layers, taps_count - 1, row_dev, channels), BF),
            V((layers, block), F32),
            V((layers, heads_dev), F32),
            V((layers, heads_dev), F32),
            V((layers, heads_dev), F32),
            V((layers, taps_count, channels), F32),
            V((layers, channels), F32),
            pltpu.SMEM((2, 1), jnp.int32),
            V((groups, steps, row_dev, block), BF),
            V((both, LANES), F32),
            V((groups, both, LANES), F32),
            V((rows, block), F32),
            V((rows, LANES), F32),
            V((layers, both, channels), F32),
            V((n_heads, channels), BF),
            V((2 * rows, 2 * block), BF),
            V((rows, block), F32),
            V((layers, 2, half, both, mix_width + LANES), F32),
            V((layers, half, both, mix_width + LANES), F32),
            V((layers, half, both, mix_width + LANES), F32),
            V((layers, half, both, mix_width + LANES), F32),
            V((layers, n_in, 2, half, 2 * both, chunk_in), BF),
            V((layers, n_in, half, 2 * both, chunk_in), BF),
            V((layers, n_in, half, 2 * both, chunk_in), BF),
            V((layers, n_in, half, 2 * both, chunk_in), BF),
            V((layers, n_in, both, chunk_in), BF),
            V((layers, n_in, groups, both, chunk_in), BF),
            V((layers, n_out, rows, chunk_out), BF),
            V((layers, n_out, parts, rows, chunk_out), BF),
            V((groups, both, block), BF),
            V((share, both, block), BF),
            V((n_out, groups, both, chunk_out), BF),
            V((n_out, share, parts, both, chunk_out), BF),
            V((n_in, rows, chunk_in), F32),
            dma((layers, 3)),
            dma((layers, n_in)),
            dma((9,)),
            dma,
            dma((groups,)),
            dma((groups,)),
            dma((groups,)),
            dma((groups,)),
            dma((layers,)),
            dma((layers,)),
            dma((layers, half)),
            dma((layers, half)),
            dma((layers, n_in)),
            dma((layers, n_in)),
            dma((layers, n_in, half)),
            dma((layers, n_in, half)),
            dma((layers, n_in, groups)),
            dma((layers, n_in, groups)),
            dma((layers, n_out, parts)),
            dma((layers, n_out, parts)),
            dma((groups,)),
            dma((share,)),
            dma((n_out, groups)),
            dma((n_out, share, parts)),
        ],
        compiler_params=pltpu.CompilerParams(
            collective_id=0, has_side_effects=True, vmem_limit_bytes=60 * 2**20
        ),
    )(
        embeds, conv, norm_gain, dt_bias, a_log, skip_gain, conv_weight, conv_bias, leave_row, arrive_from,
        state, in_weight, group_weight, out_weight,
    )


def solution(mesh):
    placed = (
        P(None, "grp", None),
        P(None, "grp", "tp", None, None),
        P(None, "grp", None, "tp"),
        P(),
        P(None, "grp", None, "tp"),
        P(None, "grp", None),
        P(None, "tp"),
        P(None, "tp"),
        P(None, "tp"),
        P(None, None, "tp"),
        P(None, "tp"),
        P(None, "tp", "grp"),
        P("grp"),
        P("grp"),
    )
    return jax.shard_map(
        local, mesh=mesh, in_specs=placed, out_specs=P(None, "grp", "tp"), check_vma=False
    )
```

```python
import functools

import jax
import jax.numpy as jnp
from jax import lax
from jax.experimental import pallas as pl
from jax.experimental.pallas import tpu as pltpu
from jax.sharding import PartitionSpec as P

F32 = jnp.float32
BF = jnp.bfloat16
LANES = 128


def iota(shape, dim):
    return lax.broadcasted_iota(jnp.int32, shape, dim)


def mm(a, b):
    return jnp.dot(a, b, preferred_element_type=F32)


def silu(v):
    return v / (1.0 + jnp.exp(-v))


def one_hot(cond):
    return cond.astype(F32).astype(BF)


def remote(src, dst, send_sem, recv_sem, device):
    return pltpu.make_async_remote_copy(
        src_ref=src,
        dst_ref=dst,
        send_sem=send_sem,
        recv_sem=recv_sem,
        device_id=device,
        device_id_type=pl.DeviceIdType.MESH,
    )


def far_first(me, n):
    upper = (2 * me) // n
    order = []
    for k in range(n - 1):
        down = n - 1 - k
        down = down - (me - down + n) // n
        up = k + (k - me + n) // n
        order.append(down + upper * (up - down))
    return order


def exact_mm(values, hot):
    rest = values
    total = jnp.zeros((values.shape[0], hot.shape[1]), F32)
    for _ in range(3):
        piece = rest.astype(BF)
        rest = rest - piece.astype(F32)
        total = total + mm(piece, hot)
    return total


def kernel(
    groups, parts, heads_dev, head_dim, chunk_in, chunk_out,
    emb, conv, gain, dt_bias, a_log, skip, taps, cbias, leave, arrive, state, w_in, w_grp, w_out,
    out,
    win_v, wg_v, wout_v, st_v,
    conv_v, gain_v, bias_v, rate_v, skip_v, taps_v, cbias_v, who,
    emb_r, info, info_r, e32, info32, pre, sel, lhs, hxs,
    m_send, m_pair, m_z, m_recv, a_send, a_pair, a_z, a_recv,
    b_send, b_recv, c_send, c_recv, h_send, h_recv, p_send, p_recv, gat,
    load_sem, in_sem, small_sem, own_sem, es_sem, er_sem, is_sem, ir_sem, mps_sem, mpr_sem, ms_sem, mr_sem,
    aps_sem, apr_sem, as_sem, ar_sem,
    bs_sem, br_sem, cs_sem, cr_sem, hs_sem, hr_sem, ps_sem, pr_sem,
):
    g = lax.axis_index("grp")
    t = lax.axis_index("tp")
    steps, row_dev, width = emb.shape
    layers = gain.shape[0]
    block = width // groups
    both = steps * row_dev
    rows = groups * both
    channels = taps.shape[2]
    taps_count = taps.shape[1]
    state_dim = st_v.shape[3]
    mix_width = wg_v.shape[2]
    n_in = channels // chunk_in
    n_out = block // chunk_out
    share = groups // parts
    half = groups // 2
    core = lax.rem(g, 2)
    chip = g // 2
    partner = g + 1 - 2 * core
    owner = g // share
    w_pairs = w_in.reshape(layers, 2 * block, channels)

    barrier = pltpu.get_barrier_semaphore()
    for d in range(1, groups):
        pl.semaphore_signal(
            barrier, inc=1, device_id={"grp": lax.rem(g + d, groups)},
            device_id_type=pl.DeviceIdType.MESH,
        )
    for d in range(1, parts):
        pl.semaphore_signal(
            barrier, inc=1, device_id={"tp": lax.rem(t + d, parts)},
            device_id_type=pl.DeviceIdType.MESH,
        )

    def arrived(ref, sem):
        remote(ref, ref, sem, sem, {"grp": partner}).wait_recv()

    def left(ref, sem):
        remote(ref, ref, sem, sem, {"grp": partner}).wait_send()

    far_chips = far_first(chip, half)
    far_peers = [2 * to + c for to in far_chips for c in range(2)] + [partner]

    def columns(who_):
        return pl.ds(pl.multiple_of(who_ * block, block), block)

    loads = {}

    def load(name, src, dst, sem):
        loads[name] = pltpu.make_async_copy(src, dst, sem)
        loads[name].start()

    load("leave", leave, who.at[0], small_sem.at[0])
    load("arrive", arrive, who.at[1], small_sem.at[1])
    load("emb", emb.at[:, :, columns(g)], emb_r.at[g], own_sem)
    load("gain", gain.at[:, columns(g)], gain_v, small_sem.at[2])
    load("bias", dt_bias, bias_v, small_sem.at[3])
    load("rate", a_log, rate_v, small_sem.at[4])
    load("skip", skip, skip_v, small_sem.at[5])
    load("taps", taps, taps_v, small_sem.at[6])
    load("cbias", cbias, cbias_v, small_sem.at[7])
    load("conv", conv, conv_v, small_sem.at[8])

    def load_in(l):
        load((l, "grp"), w_grp.at[l], wg_v.at[l], load_sem.at[l, 0])
        for c in range(n_in):
            cols = slice(c * chunk_in, (c + 1) * chunk_in)
            load((l, c), w_pairs.at[l, :, cols], win_v.at[l, :, cols], in_sem.at[l, c])

    def load_rest(l):
        load((l, "state"), state.at[l], st_v.at[l], load_sem.at[l, 1])
        load((l, "out"), w_out.at[l], wout_v.at[l], load_sem.at[l, 2])

    load_in(0)
    loads["leave"].wait()
    loads["arrive"].wait()
    first_half = iota((both, LANES), 1) < LANES // 2
    info[...] = jnp.where(first_half, who[0, 0].astype(F32), who[1, 0].astype(F32))

    pl.semaphore_wait(barrier, groups - 1 + parts - 1)

    for peer in far_peers:
        remote(emb.at[:, :, columns(peer)], emb_r.at[g], es_sem, er_sem, {"grp": peer}).start()
        remote(info, info_r.at[g], is_sem, ir_sem, {"grp": peer}).start()
    info_r[g] = info[...]
    load_rest(0)
    for l in range(1, layers):
        load_in(l)
        load_rest(l)

    n_heads = sel.shape[0]
    sel[...] = one_hot(
        iota((n_heads, channels), 0) == t * heads_dev + iota((n_heads, channels), 1) // head_dim
    )
    own_head = one_hot(iota((heads_dev, channels), 1) // head_dim == iota((heads_dev, channels), 0))
    place = one_hot(iota((heads_dev, n_heads), 1) == t * heads_dev + iota((heads_dev, n_heads), 0))
    spread = one_hot(iota((LANES, 2 * LANES), 1) // 2 == iota((LANES, 2 * LANES), 0))
    even = lax.rem(iota((rows, 2 * LANES), 1), 2) == 0
    for name in ("bias", "rate", "skip", "cbias", "conv", "taps"):
        loads[name].wait()
    bias_all = exact_mm(bias_v[...], place)
    rate_all = exact_mm(jnp.exp(rate_v[...]), place)
    skip_all = exact_mm(skip_v[...], own_head)
    for l in range(layers):
        for s in range(steps):
            total = jnp.zeros((row_dev, channels), F32)
            for k in range(taps_count - 1):
                if s + k <= taps_count - 2:
                    total = total + conv_v[l, s + k].astype(F32) * taps_v[l, k : k + 1, :]
            pre[l, s * row_dev : (s + 1) * row_dev, :] = total + cbias_v[l : l + 1, :]

    loads["gain"].wait()
    loads["emb"].wait()
    arrived(info_r.at[0 : groups - 1], ir_sem)
    arrived(emb_r.at[0 : groups - 1], er_sem)
    for i in range(groups):
        for s in range(steps):
            e32[i * both + s * row_dev : i * both + (s + 1) * row_dev, :] = emb_r[i, s].astype(F32)
        info32[i * both : (i + 1) * both, :] = info_r[i]

    square_shape = (rows, rows)
    row_i = iota(square_shape, 0)
    col_i = iota(square_shape, 1)
    on_diag = row_i == col_i
    leave_of_row = jnp.broadcast_to(info32[:, 0:1], square_shape)
    from_of_row = jnp.broadcast_to(info32[:, LANES // 2 : LANES // 2 + 1], square_shape)
    leave_of_col = jnp.sum(jnp.where(on_diag, leave_of_row, 0.0), axis=0, keepdims=True)
    from_of_col = jnp.sum(jnp.where(on_diag, from_of_row, 0.0), axis=0, keepdims=True)
    slot_row = lax.rem(row_i, row_dev).astype(F32)
    slot_col = lax.rem(col_i, row_dev).astype(F32)
    step_row = lax.rem(row_i // row_dev, steps)
    step_col = lax.rem(col_i // row_dev, steps)
    group_row = (row_i // both).astype(F32)
    group_col = (col_i // both).astype(F32)
    diag = jnp.where(on_diag, 1.0, 0.0)
    same_step = jnp.where(step_row == step_col, 1.0, 0.0)
    hit = jnp.where(group_col == from_of_row, same_step, 0.0) * jnp.where(slot_col == leave_of_col, 1.0, 0.0)
    moved_row = jnp.where(slot_row == leave_of_row, hit, diag)
    hit_t = jnp.where(group_row == from_of_col, same_step, 0.0) * jnp.where(slot_row == leave_of_row, 1.0, 0.0)
    moved_col = jnp.where(slot_col == leave_of_col, hit_t, diag)
    to_slot = [jnp.where(step_row >= n, moved_row, diag).astype(BF) for n in range(1, steps)]
    to_home = [jnp.where(step_col >= n, moved_col, diag).astype(BF) for n in range(1, steps)]

    start = e32[...]
    for hop in to_home:
        start = mm(hop, start.astype(BF))
    hxs[...] = start

    sends = [(info_r.at[0 : groups - 1], is_sem), (emb_r.at[0 : groups - 1], es_sem)]
    row_step = iota((both, chunk_in), 0) // row_dev
    slot16 = lax.rem(iota((2 * both, channels), 0), row_dev)

    def repeat_step(v, e):
        return jnp.concatenate([v[e * row_dev : (e + 1) * row_dev]] * steps, axis=0)

    for l in range(layers):
        last = l == layers - 1
        done = sends
        sends = []
        hx = hxs[...]
        gained = (hx * gain_v[l : l + 1, :]).astype(BF)
        loads[l, "grp"].wait()
        mix = mm(gained, wg_v[l])
        square = jnp.broadcast_to(jnp.sum(hx * hx, axis=1, keepdims=True), (rows, LANES))
        for i in range(groups):
            m_send[l, i % 2, i // 2, :, :mix_width] = mix[i * both : (i + 1) * both].astype(BF)
            m_send[l, i % 2, i // 2, :, mix_width:] = square[i * both : (i + 1) * both].astype(BF)
        remote(m_send.at[l, 1 - core], m_pair.at[l], mps_sem.at[l], mpr_sem.at[l], {"grp": partner}).start()
        sends.append((m_pair.at[l], mps_sem.at[l]))
        for j in range(block // LANES):
            wide = mm(gained[:, j * LANES : (j + 1) * LANES], spread)
            lhs[0:rows, 2 * j * LANES : 2 * (j + 1) * LANES] = jnp.where(even, wide, 0.0).astype(BF)
            lhs[rows : 2 * rows, 2 * j * LANES : 2 * (j + 1) * LANES] = jnp.where(even, 0.0, wide).astype(BF)
        for c in range(n_in + 1):
            if c < n_in:
                loads[l, c].wait()
                acc = mm(lhs[...], win_v[l, :, c * chunk_in : (c + 1) * chunk_in])
                for i in range(groups):
                    a_send[l, c, i % 2, i // 2] = jnp.concatenate(
                        [acc[i * both : (i + 1) * both], acc[rows + i * both : rows + (i + 1) * both]], axis=0
                    ).astype(BF)
                remote(
                    a_send.at[l, c, 1 - core], a_pair.at[l, c], aps_sem.at[l], apr_sem.at[l, c], {"grp": partner}
                ).start()
            if c == 0:
                arrived(m_pair.at[l], mpr_sem.at[l])
                m_z[l] = (m_send[l, core].astype(F32) + m_pair[l].astype(F32)).astype(BF)
                for to in far_chips:
                    remote(
                        m_z.at[l, to], m_recv.at[l, chip], ms_sem.at[l], mr_sem.at[l], {"grp": 2 * to + core}
                    ).start()
                m_recv[l, chip] = m_z[l, chip]
            else:
                e = c - 1
                arrived(a_pair.at[l, e], apr_sem.at[l, e])
                a_z[l, e] = (a_send[l, e, core].astype(F32) + a_pair[l, e].astype(F32)).astype(BF)
                for to in far_chips:
                    remote(
                        a_z.at[l, e, to], a_recv.at[l, e, chip], as_sem.at[l], ar_sem.at[l, e],
                        {"grp": 2 * to + core},
                    ).start()
                a_recv[l, e, chip] = a_z[l, e, chip]
        sends.append((a_pair.at[l], aps_sem.at[l]))
        sends.append((m_recv.at[l, 0 : half - 1], ms_sem.at[l]))
        sends.append((a_recv.at[l, :, 0 : half - 1], as_sem.at[l]))

        if last:
            final = hx.astype(BF)
            for hop in to_slot:
                final = mm(hop, final).astype(BF)
            final = final.astype(F32)
            for i in range(groups):
                h_send[i] = final[i * both : (i + 1) * both].astype(BF)

            @pl.when(owner == t)
            def _():
                for peer in far_peers:
                    remote(
                        h_send.at[peer], h_recv.at[lax.rem(g, share)], hs_sem, hr_sem, {"grp": peer}
                    ).start()
                h_recv[lax.rem(g, share)] = h_send[g]

        for ref, sem in done:
            left(ref, sem)
        arrived(m_recv.at[l, 0 : half - 1], mr_sem.at[l])
        msum = m_recv[l, 0].astype(F32)
        for i in range(1, half):
            msum = msum + m_recv[l, i].astype(F32)
        scale = lax.rsqrt(msum[:, mix_width : mix_width + 1] / width + 1e-05)
        b_mat = msum[:, :state_dim] * scale
        c_mat = msum[:, state_dim : 2 * state_dim] * scale
        pre_dt = msum[:, 2 * state_dim : mix_width] * scale + bias_all[l : l + 1, :]
        step_size = jnp.maximum(pre_dt, 0.0) + jnp.log1p(jnp.exp(-jnp.abs(pre_dt)))
        decay = jnp.exp(-step_size * rate_all[l : l + 1, :])
        pieces = []
        for v in (step_size, decay):
            hi = v.astype(BF).astype(F32)
            pieces += [hi, v - hi]
        wide = mm(jnp.concatenate(pieces, axis=0).astype(BF), sel[...])
        step_ch = wide[0:both] + wide[both : 2 * both]
        decay_ch = wide[2 * both : 3 * both] + wide[3 * both : 4 * both]
        bc = [jnp.sum(repeat_step(b_mat, e) * c_mat, axis=1, keepdims=True) for e in range(steps)]
        c_hi = c_mat.astype(BF).astype(F32)
        c_both = jnp.concatenate([c_hi, c_mat - c_hi], axis=0).astype(BF)
        loads[l, "state"].wait()
        total = jnp.zeros((2 * both, channels), F32)
        for r in range(row_dev):
            got = lax.dot_general(
                c_both, st_v[l, r], (((1,), (1,)), ((), ())), preferred_element_type=F32
            )
            total = jnp.where(slot16 == r, got, total)
        state_y = total[0:both] + total[both : 2 * both]

        for c in range(n_in):
            cols = slice(c * chunk_in, (c + 1) * chunk_in)
            arrived(a_recv.at[l, c, 0 : half - 1], ar_sem.at[l, c])
            asum = a_recv[l, c, 0].astype(F32)
            for i in range(1, half):
                asum = asum + a_recv[l, c, i].astype(F32)
            x = (asum[0:both] * scale).astype(BF).astype(F32)
            z = asum[both : 2 * both] * scale
            conv_sum = pre[l, :, cols] + x * taps_v[l, taps_count - 1 : taps_count, cols]
            for e in range(1, steps):
                tap = taps_count - 1 - e
                if tap >= 0:
                    before = jnp.concatenate(
                        [jnp.zeros((e * row_dev, chunk_in), F32), x[: both - e * row_dev]], axis=0
                    )
                    conv_sum = conv_sum + before * taps_v[l, tap : tap + 1, cols]
            xc = silu(conv_sum)
            dtx = step_ch[:, cols] * xc
            dec = decay_ch[:, cols]
            acc_y = state_y[:, cols]
            for e in range(steps):
                later = repeat_step(dec, e) * acc_y + repeat_step(dtx, e) * bc[e]
                acc_y = later if e == 0 else jnp.where(row_step >= e, later, acc_y)
            gated = ((acc_y + skip_all[l : l + 1, cols] * xc) * silu(z)).astype(BF)
            b_send[l, c] = gated
            b_recv[l, c, g] = gated
            for peer in far_peers:
                remote(
                    b_send.at[l, c], b_recv.at[l, c, g], bs_sem.at[l], br_sem.at[l, c], {"grp": peer}
                ).start()
        sends.append((b_recv.at[l, :, 0 : groups - 1], bs_sem.at[l]))

        loads[l, "out"].wait()
        gated_all = []
        for c in range(n_in):
            arrived(b_recv.at[l, c, 0 : groups - 1], br_sem.at[l, c])
            for i in range(groups):
                gat[c, i * both : (i + 1) * both, :] = b_recv[l, c, i].astype(F32)
            part = gat[c].astype(BF)
            if last:
                for hop in to_slot:
                    part = mm(hop, part).astype(BF)
            gated_all.append(part)
        gated_all = jnp.concatenate(gated_all, axis=1)

        for n in range(n_out):
            cols = slice(n * chunk_out, (n + 1) * chunk_out)
            part = mm(gated_all, wout_v[l, :, cols])
            if not last:
                c_send[l, n] = part.astype(BF)
                c_recv[l, n, t] = c_send[l, n]
                for d in range(parts - 1, 0, -1):
                    remote(
                        c_send.at[l, n], c_recv.at[l, n, t], cs_sem.at[l], cr_sem.at[l, n],
                        {"tp": lax.rem(t + d, parts)},
                    ).start()
            else:
                spot = lax.rem(g, share) * parts + t
                for i in range(groups):
                    p_send[n, i] = part[i * both : (i + 1) * both].astype(BF)
                for peer in far_peers:
                    remote(
                        p_send.at[n, peer], p_recv.at[n, spot], ps_sem, pr_sem.at[n], {"grp": peer, "tp": owner}
                    ).start()

                @pl.when(owner == t)
                def _(n=n):
                    p_recv[n, spot] = p_send[n, g]

                @pl.when(owner != t)
                def _(n=n):
                    remote(
                        p_send.at[n, g], p_recv.at[n, spot], ps_sem, pr_sem.at[n], {"grp": g, "tp": owner}
                    ).start()

        if not last:
            sends.append((c_recv.at[l, :, 0 : parts - 1], cs_sem.at[l]))
            for n in range(n_out):
                arrived(c_recv.at[l, n, 0 : parts - 1], cr_sem.at[l, n])
                dsum = c_recv[l, n, 0].astype(F32)
                for i in range(1, parts):
                    dsum = dsum + c_recv[l, n, i].astype(F32)
                cols = slice(n * chunk_out, (n + 1) * chunk_out)
                hxs[:, cols] = (hxs[:, cols] + dsum.astype(BF).astype(F32)).astype(BF).astype(F32)

    for ref, sem in sends:
        left(ref, sem)

    @pl.when(owner == t)
    def _():
        left(h_send.at[0 : groups - 1], hs_sem)
        left(p_send.at[:, 0 : groups - 1], ps_sem)
        if share > 1:
            arrived(h_recv.at[0 : share - 1], hr_sem)

    @pl.when(owner != t)
    def _():
        left(p_send, ps_sem)
        arrived(h_recv, hr_sem)

    for n in range(n_out):

        @pl.when(owner == t)
        def _(n=n):
            arrived(p_recv.at[n, 0 : share * parts - 1], pr_sem.at[n])

        @pl.when(owner != t)
        def _(n=n):
            arrived(p_recv.at[n], pr_sem.at[n])

        for j in range(share):
            dsum = p_recv[n, j * parts].astype(F32)
            for i in range(1, parts):
                dsum = dsum + p_recv[n, j * parts + i].astype(F32)
            cols = slice(n * chunk_out, (n + 1) * chunk_out)
            result = h_recv[j, :, cols].astype(F32) + dsum.astype(BF).astype(F32)
            for s in range(steps):
                out[s, :, j * block + n * chunk_out : j * block + (n + 1) * chunk_out] = result[
                    s * row_dev : (s + 1) * row_dev
                ].astype(BF)


def local(
    embeds, ssm_state, conv_state, norm_gain, in_weight, group_weight, dt_bias, a_log,
    skip_gain, conv_weight, conv_bias, out_weight, leave_row, arrive_from,
):
    groups = lax.axis_size("grp")
    parts = lax.axis_size("tp")
    steps, row_dev, width = embeds.shape
    layers, _, heads_dev, head_dim, state_dim = ssm_state.shape
    block = in_weight.shape[1]
    channels = in_weight.shape[3]
    mix_width = group_weight.shape[2]
    n_heads = mix_width - 2 * state_dim
    taps_count = conv_weight.shape[1]
    both = steps * row_dev
    rows = groups * both
    share = groups // parts
    half = groups // 2
    chunk_in = min(512, channels)
    chunk_out = min(512, block)
    n_in = channels // chunk_in
    n_out = block // chunk_out

    state = ssm_state.reshape(layers, row_dev, channels, state_dim)
    conv = conv_state.transpose(0, 2, 1, 3)
    vm = pl.BlockSpec(memory_space=pltpu.VMEM)
    anywhere = pl.BlockSpec(memory_space=pl.ANY)
    dma = pltpu.SemaphoreType.DMA
    V = pltpu.VMEM
    return pl.pallas_call(
        functools.partial(kernel, groups, parts, heads_dev, head_dim, chunk_in, chunk_out),
        out_shape=jax.ShapeDtypeStruct((steps, row_dev, width // parts), BF),
        in_specs=[anywhere] * 14,
        out_specs=vm,
        scratch_shapes=[
            V((layers, 2 * block, channels), BF),
            V((layers, block, mix_width), BF),
            V((layers, channels, block), BF),
            V((layers, row_dev, channels, state_dim), BF),
            V((layers, taps_count - 1, row_dev, channels), BF),
            V((layers, block), F32),
            V((layers, heads_dev), F32),
            V((layers, heads_dev), F32),
            V((layers, heads_dev), F32),
            V((layers, taps_count, channels), F32),
            V((layers, channels), F32),
            pltpu.SMEM((2, 1), jnp.int32),
            V((groups, steps, row_dev, block), BF),
            V((both, LANES), F32),
            V((groups, both, LANES), F32),
            V((rows, block), F32),
            V((rows, LANES), F32),
            V((layers, both, channels), F32),
            V((n_heads, channels), BF),
            V((2 * rows, 2 * block), BF),
            V((rows, block), F32),
            V((layers, 2, half, both, mix_width + LANES), BF),
            V((layers, half, both, mix_width + LANES), BF),
            V((layers, half, both, mix_width + LANES), BF),
            V((layers, half, both, mix_width + LANES), BF),
            V((layers, n_in, 2, half, 2 * both, chunk_in), BF),
            V((layers, n_in, half, 2 * both, chunk_in), BF),
            V((layers, n_in, half, 2 * both, chunk_in), BF),
            V((layers, n_in, half, 2 * both, chunk_in), BF),
            V((layers, n_in, both, chunk_in), BF),
            V((layers, n_in, groups, both, chunk_in), BF),
            V((layers, n_out, rows, chunk_out), BF),
            V((layers, n_out, parts, rows, chunk_out), BF),
            V((groups, both, block), BF),
            V((share, both, block), BF),
            V((n_out, groups, both, chunk_out), BF),
            V((n_out, share * parts, both, chunk_out), BF),
            V((n_in, rows, chunk_in), F32),
            dma((layers, 3)),
            dma((layers, n_in)),
            dma((9,)),
            dma,
            dma,
            dma,
            dma,
            dma,
            dma((layers,)),
            dma((layers,)),
            dma((layers,)),
            dma((layers,)),
            dma((layers,)),
            dma((layers, n_in)),
            dma((layers,)),
            dma((layers, n_in)),
            dma((layers,)),
            dma((layers, n_in)),
            dma((layers,)),
            dma((layers, n_out)),
            dma,
            dma,
            dma,
            dma((n_out,)),
        ],
        compiler_params=pltpu.CompilerParams(
            collective_id=0, has_side_effects=True, vmem_limit_bytes=60 * 2**20
        ),
    )(
        embeds, conv, norm_gain, dt_bias, a_log, skip_gain, conv_weight, conv_bias, leave_row, arrive_from,
        state, in_weight, group_weight, out_weight,
    )


def solution(mesh):
    placed = (
        P(None, "grp", None),
        P(None, "grp", "tp", None, None),
        P(None, "grp", None, "tp"),
        P(),
        P(None, "grp", None, "tp"),
        P(None, "grp", None),
        P(None, "tp"),
        P(None, "tp"),
        P(None, "tp"),
        P(None, None, "tp"),
        P(None, "tp"),
        P(None, "tp", "grp"),
        P("grp"),
        P("grp"),
    )
    return jax.shard_map(
        local, mesh=mesh, in_specs=placed, out_specs=P(None, "grp", "tp"), check_vma=False
    )
```

```python
import functools

import jax
import jax.numpy as jnp
from jax import lax
from jax.experimental import pallas as pl
from jax.experimental.pallas import tpu as pltpu
from jax.sharding import PartitionSpec as P

F32 = jnp.float32
BF = jnp.bfloat16
LANES = 128


def iota(shape, dim):
    return lax.broadcasted_iota(jnp.int32, shape, dim)


def mm(a, b):
    return jnp.dot(a, b, preferred_element_type=F32)


def silu(v):
    return v / (1.0 + jnp.exp(-v))


def one_hot(cond):
    return cond.astype(F32).astype(BF)


def remote(src, dst, send_sem, recv_sem, device):
    return pltpu.make_async_remote_copy(
        src_ref=src,
        dst_ref=dst,
        send_sem=send_sem,
        recv_sem=recv_sem,
        device_id=device,
        device_id_type=pl.DeviceIdType.MESH,
    )


def far_first(me, n):
    upper = (2 * me) // n
    order = []
    for k in range(n - 1):
        down = n - 1 - k
        down = down - (me - down + n) // n
        up = k + (k - me + n) // n
        order.append(down + upper * (up - down))
    return order


def exact_mm(values, hot):
    rest = values
    total = jnp.zeros((values.shape[0], hot.shape[1]), F32)
    for _ in range(3):
        piece = rest.astype(BF)
        rest = rest - piece.astype(F32)
        total = total + mm(piece, hot)
    return total


def kernel(
    groups, parts, heads_dev, head_dim, chunk_in, chunk_out,
    emb, conv, gain, dt_bias, a_log, skip, taps, cbias, leave, arrive, state, w_in, w_grp, w_out,
    out,
    win_v, wg_v, wout_v, st_v,
    conv_v, gain_v, bias_v, rate_v, skip_v, taps_v, cbias_v, who,
    emb_r, info, info_r, e32, info32, pre, sel, lhs, hxs, keep_d, keep_u, keep_x, keep_b, y_v,
    m_send, m_pair, m_z, m_recv, a_send, a_pair, a_z, a_recv,
    b_send, b_recv, c_send, c_recv, h_send, h_recv, p_send, p_recv, gat, gat_p, gat_h,
    load_sem, in_sem, small_sem, own_sem, es_sem, er_sem, is_sem, ir_sem, mps_sem, mpr_sem, ms_sem, mr_sem,
    aps_sem, apr_sem, as_sem, ar_sem,
    bs_sem, br_sem, cs_sem, cr_sem, hs_sem, hr_sem, ps_sem, pr_sem,
):
    g = lax.axis_index("grp")
    t = lax.axis_index("tp")
    steps, row_dev, width = emb.shape
    layers = gain.shape[0]
    block = width // groups
    rows = groups * row_dev
    pair = 2 * row_dev
    channels = taps.shape[2]
    taps_count = taps.shape[1]
    state_dim = st_v.shape[3]
    mix_width = wg_v.shape[2]
    n_in = channels // chunk_in
    n_out = block // chunk_out
    share = groups // parts
    half = groups // 2
    core = lax.rem(g, 2)
    chip = g // 2
    partner = g + 1 - 2 * core
    owner = g // share
    w_pairs = w_in.reshape(layers, 2 * block, channels)

    barrier = pltpu.get_barrier_semaphore()
    for d in range(1, groups):
        pl.semaphore_signal(
            barrier, inc=1, device_id={"grp": lax.rem(g + d, groups)},
            device_id_type=pl.DeviceIdType.MESH,
        )
    for d in range(1, parts):
        pl.semaphore_signal(
            barrier, inc=1, device_id={"tp": lax.rem(t + d, parts)},
            device_id_type=pl.DeviceIdType.MESH,
        )

    def arrived(ref, sem):
        remote(ref, ref, sem, sem, {"grp": partner}).wait_recv()

    def left(ref, sem):
        remote(ref, ref, sem, sem, {"grp": partner}).wait_send()

    far_chips = far_first(chip, half)
    far_peers = [2 * to + c for to in far_chips for c in range(2)] + [partner]

    def columns(who_):
        return pl.ds(pl.multiple_of(who_ * block, block), block)

    loads = {}

    def load(name, src, dst, sem):
        loads[name] = pltpu.make_async_copy(src, dst, sem)
        loads[name].start()

    load("leave", leave, who.at[0], small_sem.at[0])
    load("arrive", arrive, who.at[1], small_sem.at[1])
    load("emb", emb.at[:, :, columns(g)], emb_r.at[g], own_sem)
    load("gain", gain.at[:, columns(g)], gain_v, small_sem.at[2])
    load("bias", dt_bias, bias_v, small_sem.at[3])
    load("rate", a_log, rate_v, small_sem.at[4])
    load("skip", skip, skip_v, small_sem.at[5])
    load("taps", taps, taps_v, small_sem.at[6])
    load("cbias", cbias, cbias_v, small_sem.at[7])
    load("conv", conv, conv_v, small_sem.at[8])

    def load_in(l):
        load((l, "grp"), w_grp.at[l], wg_v.at[l], load_sem.at[l, 0])
        for c in range(n_in):
            cols = slice(c * chunk_in, (c + 1) * chunk_in)
            load((l, c), w_pairs.at[l, :, cols], win_v.at[l, :, cols], in_sem.at[l, c])

    def load_rest(l):
        load((l, "state"), state.at[l], st_v.at[l], load_sem.at[l, 1])
        load((l, "out"), w_out.at[l], wout_v.at[l], load_sem.at[l, 2])

    load_in(0)
    loads["leave"].wait()
    loads["arrive"].wait()
    first_half = iota((row_dev, LANES), 1) < LANES // 2
    info[...] = jnp.where(first_half, who[0, 0].astype(F32), who[1, 0].astype(F32))

    pl.semaphore_wait(barrier, groups - 1 + parts - 1)

    for peer in far_peers:
        remote(emb.at[:, :, columns(peer)], emb_r.at[g], es_sem, er_sem, {"grp": peer}).start()
        remote(info, info_r.at[g], is_sem, ir_sem, {"grp": peer}).start()
    info_r[g] = info[...]
    load_rest(0)
    for l in range(1, layers):
        load_in(l)
        load_rest(l)

    n_heads = sel.shape[0]
    sel[...] = one_hot(
        iota((n_heads, channels), 0) == t * heads_dev + iota((n_heads, channels), 1) // head_dim
    )
    own_head = one_hot(iota((heads_dev, channels), 1) // head_dim == iota((heads_dev, channels), 0))
    place = one_hot(iota((heads_dev, n_heads), 1) == t * heads_dev + iota((heads_dev, n_heads), 0))
    spread = one_hot(iota((LANES, 2 * LANES), 1) // 2 == iota((LANES, 2 * LANES), 0))
    own_half = lax.rem(iota((2 * rows, 2 * LANES), 1), 2) == lax.rem(
        iota((2 * rows, 2 * LANES), 0) // row_dev, 2
    )
    dup_row = iota((2 * rows, rows), 0)
    dup = one_hot(iota((2 * rows, rows), 1) == (dup_row // pair) * row_dev + lax.rem(dup_row, row_dev))
    und_col = iota((rows, 2 * rows), 1)
    und_row = iota((rows, 2 * rows), 0)
    undup = one_hot(und_col == (und_row // row_dev) * pair + lax.rem(und_row, row_dev))
    for name in ("bias", "rate", "skip", "cbias", "conv", "taps"):
        loads[name].wait()
    bias_all = exact_mm(bias_v[...], place)
    rate_all = exact_mm(jnp.exp(rate_v[...]), place)
    skip_all = exact_mm(skip_v[...], own_head)
    for l in range(layers):
        for s in range(steps):
            total = jnp.zeros((row_dev, channels), F32)
            for k in range(taps_count - 1):
                if s + k <= taps_count - 2:
                    total = total + conv_v[l, s + k].astype(F32) * taps_v[l, k : k + 1, :]
            pre[l, s] = total + cbias_v[l : l + 1, :]

    loads["gain"].wait()
    loads["emb"].wait()
    arrived(info_r.at[0 : groups - 1], ir_sem)
    arrived(emb_r.at[0 : groups - 1], er_sem)
    for i in range(groups):
        for s in range(steps):
            e32[s, i * row_dev : (i + 1) * row_dev, :] = emb_r[i, s].astype(F32)
        info32[i * row_dev : (i + 1) * row_dev, :] = info_r[i]

    square_shape = (rows, rows)
    row_i = iota(square_shape, 0)
    col_i = iota(square_shape, 1)
    on_diag = row_i == col_i
    leave_of_row = jnp.broadcast_to(info32[:, 0:1], square_shape)
    from_of_row = jnp.broadcast_to(info32[:, LANES // 2 : LANES // 2 + 1], square_shape)
    leave_of_col = jnp.sum(jnp.where(on_diag, leave_of_row, 0.0), axis=0, keepdims=True)
    from_of_col = jnp.sum(jnp.where(on_diag, from_of_row, 0.0), axis=0, keepdims=True)
    slot_row = lax.rem(row_i, row_dev).astype(F32)
    slot_col = lax.rem(col_i, row_dev).astype(F32)
    group_row = (row_i // row_dev).astype(F32)
    group_col = (col_i // row_dev).astype(F32)
    diag = jnp.where(on_diag, 1.0, 0.0)
    hit = jnp.where(group_col == from_of_row, 1.0, 0.0) * jnp.where(slot_col == leave_of_col, 1.0, 0.0)
    to_slot = jnp.where(slot_row == leave_of_row, hit, diag).astype(BF)
    hit_t = jnp.where(group_row == from_of_col, 1.0, 0.0) * jnp.where(slot_row == leave_of_row, 1.0, 0.0)
    to_home = jnp.where(slot_col == leave_of_col, hit_t, diag).astype(BF)

    for s in range(steps):
        start = e32[s].astype(BF)
        for _ in range(s):
            start = mm(to_home, start).astype(BF)
        hxs[s] = mm(dup, start)

    sends = [(info_r.at[0 : groups - 1], is_sem), (emb_r.at[0 : groups - 1], es_sem)]
    slot8 = lax.rem(iota((pair, channels), 0), row_dev)
    waiting = []

    def pass_on():
        l, s, c = waiting.pop(0)
        if c < 0:
            arrived(m_pair.at[l, s], mpr_sem.at[l, s])
            m_z[l, s] = (m_send[l, s, core].astype(F32) + m_pair[l, s].astype(F32)).astype(BF)
            for to in far_chips:
                remote(
                    m_z.at[l, s, to], m_recv.at[l, s, chip], ms_sem.at[l], mr_sem.at[l, s], {"grp": 2 * to + core}
                ).start()
            m_recv[l, s, chip] = m_z[l, s, chip]
        else:
            arrived(a_pair.at[l, s, c], apr_sem.at[l, s, c])
            a_z[l, s, c] = (a_send[l, s, c, core].astype(F32) + a_pair[l, s, c].astype(F32)).astype(BF)
            for to in far_chips:
                remote(
                    a_z.at[l, s, c, to], a_recv.at[l, s, c, chip], as_sem.at[l], ar_sem.at[l, s, c],
                    {"grp": 2 * to + core},
                ).start()
            a_recv[l, s, c, chip] = a_z[l, s, c, chip]

    def enter(l, s):
        hx = hxs[s]
        gained = (hx * gain_v[l : l + 1, :]).astype(BF)
        if s == 0:
            loads[l, "grp"].wait()
        mix = mm(gained, wg_v[l])
        square = jnp.broadcast_to(jnp.sum(hx * hx, axis=1, keepdims=True), (2 * rows, LANES))
        for i in range(groups):
            m_send[l, s, i % 2, i // 2, :, :mix_width] = mix[i * pair : i * pair + row_dev].astype(BF)
            m_send[l, s, i % 2, i // 2, :, mix_width:] = square[i * pair : i * pair + row_dev].astype(BF)
        remote(
            m_send.at[l, s, 1 - core], m_pair.at[l, s], mps_sem.at[l], mpr_sem.at[l, s], {"grp": partner}
        ).start()
        waiting.append((l, s, -1))
        for j in range(block // LANES):
            wide = mm(gained[:, j * LANES : (j + 1) * LANES], spread)
            lhs[s, :, 2 * j * LANES : 2 * (j + 1) * LANES] = jnp.where(own_half, wide, 0.0).astype(BF)
        for c in range(n_in):
            if s == 0:
                loads[l, c].wait()
            acc = mm(lhs[s], win_v[l, :, c * chunk_in : (c + 1) * chunk_in])
            for i in range(groups):
                a_send[l, s, c, i % 2, i // 2] = acc[i * pair : (i + 1) * pair].astype(BF)
            remote(
                a_send.at[l, s, c, 1 - core], a_pair.at[l, s, c], aps_sem.at[l], apr_sem.at[l, s, c], {"grp": partner}
            ).start()
            waiting.append((l, s, c))
            while len(waiting) > 1:
                pass_on()
        if l > 0 or s == steps - 1:
            pass_on()

    def mixer(l, s):
        arrived(m_recv.at[l, s, 0 : half - 1], mr_sem.at[l, s])
        msum = m_recv[l, s, 0].astype(F32)
        for i in range(1, half):
            msum = msum + m_recv[l, s, i].astype(F32)
        scale = lax.rsqrt(msum[:, mix_width : mix_width + 1] / width + 1e-05)
        b_mat = msum[:, :state_dim] * scale
        c_mat = msum[:, state_dim : 2 * state_dim] * scale
        keep_b[l, s] = b_mat
        pre_dt = msum[:, 2 * state_dim : mix_width] * scale + bias_all[l : l + 1, :]
        step_size = jnp.maximum(pre_dt, 0.0) + jnp.log1p(jnp.exp(-jnp.abs(pre_dt)))
        decay = jnp.exp(-step_size * rate_all[l : l + 1, :])
        pieces = []
        for v in (step_size, decay):
            hi = v.astype(BF).astype(F32)
            pieces += [hi, v - hi]
        wide = mm(jnp.concatenate(pieces, axis=0).astype(BF), sel[...])
        step_ch = wide[0:row_dev] + wide[row_dev:pair]
        keep_d[l, s] = wide[pair : pair + row_dev] + wide[pair + row_dev : 2 * pair]
        bc = [jnp.sum(keep_b[l, e] * c_mat, axis=1, keepdims=True) for e in range(s + 1)]
        c_hi = c_mat.astype(BF).astype(F32)
        c_both = jnp.concatenate([c_hi, c_mat - c_hi], axis=0).astype(BF)
        if s == 0:
            loads[l, "state"].wait()
        total = jnp.zeros((pair, channels), F32)
        for r in range(row_dev):
            got = lax.dot_general(
                c_both, st_v[l, r], (((1,), (1,)), ((), ())), preferred_element_type=F32
            )
            total = jnp.where(slot8 == r, got, total)
        y_v[...] = total[0:row_dev] + total[row_dev:pair]

        for c in range(n_in):
            cols = slice(c * chunk_in, (c + 1) * chunk_in)
            arrived(a_recv.at[l, s, c, 0 : half - 1], ar_sem.at[l, s, c])
            asum = a_recv[l, s, c, 0].astype(F32)
            for i in range(1, half):
                asum = asum + a_recv[l, s, c, i].astype(F32)
            x = (asum[0:row_dev] * scale).astype(BF).astype(F32)
            z = asum[row_dev:pair] * scale
            keep_x[l, s, :, cols] = x
            conv_sum = pre[l, s, :, cols] + x * taps_v[l, taps_count - 1 : taps_count, cols]
            for e in range(s):
                tap = taps_count - 1 + e - s
                if tap >= 0:
                    conv_sum = conv_sum + keep_x[l, e, :, cols] * taps_v[l, tap : tap + 1, cols]
            xc = silu(conv_sum)
            keep_u[l, s, :, cols] = step_ch[:, cols] * xc
            acc_y = y_v[:, cols]
            for e in range(s + 1):
                acc_y = keep_d[l, e, :, cols] * acc_y + keep_u[l, e, :, cols] * bc[e]
            gated = ((acc_y + skip_all[l : l + 1, cols] * xc) * silu(z)).astype(BF)
            b_send[l, s, c] = gated
            b_recv[l, s, c, g] = gated
            for peer in far_peers:
                remote(
                    b_send.at[l, s, c], b_recv.at[l, s, c, g], bs_sem.at[l], br_sem.at[l, s, c], {"grp": peer}
                ).start()

    def project(l, s):
        if s == 0:
            loads[l, "out"].wait()
        gated_all = []
        for c in range(n_in):
            arrived(b_recv.at[l, s, c, 0 : groups - 1], br_sem.at[l, s, c])
            for i in range(groups):
                gat[s, c, i * row_dev : (i + 1) * row_dev, :] = b_recv[l, s, c, i].astype(F32)
            part = gat[s, c].astype(BF)
            if l == layers - 1:
                for _ in range(s):
                    part = mm(to_slot, part).astype(BF)
            gated_all.append(part)
        gated_all = jnp.concatenate(gated_all, axis=1)
        for n in range(n_out):
            part = mm(gated_all, wout_v[l, :, n * chunk_out : (n + 1) * chunk_out])
            if l < layers - 1:
                c_send[l, s, n] = part.astype(BF)
                c_recv[l, s, n, t] = c_send[l, s, n]
                for d in range(parts - 1, 0, -1):
                    remote(
                        c_send.at[l, s, n], c_recv.at[l, s, n, t], cs_sem.at[l], cr_sem.at[l, s, n],
                        {"tp": lax.rem(t + d, parts)},
                    ).start()
            else:
                spot = lax.rem(g, share) * parts + t
                gat_p[...] = part
                for i in range(groups):
                    p_send[s, n, i] = gat_p[i * row_dev : (i + 1) * row_dev, :].astype(BF)
                for peer in far_peers:
                    remote(
                        p_send.at[s, n, peer], p_recv.at[s, n, spot], ps_sem, pr_sem.at[s, n],
                        {"grp": peer, "tp": owner},
                    ).start()

                @pl.when(owner == t)
                def _():
                    p_recv[s, n, spot] = p_send[s, n, g]

                @pl.when(owner != t)
                def _():
                    remote(
                        p_send.at[s, n, g], p_recv.at[s, n, spot], ps_sem, pr_sem.at[s, n],
                        {"grp": g, "tp": owner},
                    ).start()

    def update(l, s):
        for n in range(n_out):
            arrived(c_recv.at[l, s, n, 0 : parts - 1], cr_sem.at[l, s, n])
            dsum = c_recv[l, s, n, 0].astype(F32)
            for i in range(1, parts):
                dsum = dsum + c_recv[l, s, n, i].astype(F32)
            cols = slice(n * chunk_out, (n + 1) * chunk_out)
            hxs[s, :, cols] = (hxs[s, :, cols] + mm(dup, dsum.astype(BF))).astype(BF).astype(F32)

    for l in range(layers):
        for s in range(steps):
            if l > 0:
                update(l - 1, s)
            enter(l, s)
        if l == layers - 1:
            for s in range(steps):
                final = mm(undup, hxs[s].astype(BF))
                for _ in range(s):
                    final = mm(to_slot, final.astype(BF))
                gat_h[...] = final
                for i in range(groups):
                    h_send[i, s] = gat_h[i * row_dev : (i + 1) * row_dev, :].astype(BF)

            @pl.when(owner == t)
            def _():
                for peer in far_peers:
                    remote(
                        h_send.at[peer], h_recv.at[lax.rem(g, share)], hs_sem, hr_sem, {"grp": peer}
                    ).start()
                h_recv[lax.rem(g, share)] = h_send[g]

        for ref, sem in sends:
            left(ref, sem)
        for s in range(steps):
            mixer(l, s)
        for s in range(steps):
            project(l, s)
        sends = [
            (m_pair.at[l], mps_sem.at[l]),
            (a_pair.at[l], aps_sem.at[l]),
            (m_recv.at[l, :, 0 : half - 1], ms_sem.at[l]),
            (a_recv.at[l, :, :, 0 : half - 1], as_sem.at[l]),
            (b_recv.at[l, :, :, 0 : groups - 1], bs_sem.at[l]),
        ]
        if l < layers - 1:
            sends.append((c_recv.at[l, :, :, 0 : parts - 1], cs_sem.at[l]))

    for ref, sem in sends:
        left(ref, sem)

    @pl.when(owner == t)
    def _():
        left(h_send.at[0 : groups - 1], hs_sem)
        left(p_send.at[:, :, 0 : groups - 1], ps_sem)
        if share > 1:
            arrived(h_recv.at[0 : share - 1], hr_sem)

    @pl.when(owner != t)
    def _():
        left(p_send, ps_sem)
        arrived(h_recv, hr_sem)

    for s in range(steps):
        for n in range(n_out):

            @pl.when(owner == t)
            def _():
                arrived(p_recv.at[s, n, 0 : share * parts - 1], pr_sem.at[s, n])

            @pl.when(owner != t)
            def _():
                arrived(p_recv.at[s, n], pr_sem.at[s, n])

            for j in range(share):
                dsum = p_recv[s, n, j * parts].astype(F32)
                for i in range(1, parts):
                    dsum = dsum + p_recv[s, n, j * parts + i].astype(F32)
                result = h_recv[j, s, :, n * chunk_out : (n + 1) * chunk_out].astype(F32) + dsum.astype(BF).astype(F32)
                out[s, :, j * block + n * chunk_out : j * block + (n + 1) * chunk_out] = result.astype(BF)


def local(
    embeds, ssm_state, conv_state, norm_gain, in_weight, group_weight, dt_bias, a_log,
    skip_gain, conv_weight, conv_bias, out_weight, leave_row, arrive_from,
):
    groups = lax.axis_size("grp")
    parts = lax.axis_size("tp")
    steps, row_dev, width = embeds.shape
    layers, _, heads_dev, head_dim, state_dim = ssm_state.shape
    block = in_weight.shape[1]
    channels = in_weight.shape[3]
    mix_width = group_weight.shape[2]
    n_heads = mix_width - 2 * state_dim
    taps_count = conv_weight.shape[1]
    rows = groups * row_dev
    pair = 2 * row_dev
    share = groups // parts
    half = groups // 2
    chunk_in = min(1024, channels)
    chunk_out = min(512, block)
    n_in = channels // chunk_in
    n_out = block // chunk_out

    state = ssm_state.reshape(layers, row_dev, channels, state_dim)
    conv = conv_state.transpose(0, 2, 1, 3)
    vm = pl.BlockSpec(memory_space=pltpu.VMEM)
    anywhere = pl.BlockSpec(memory_space=pl.ANY)
    dma = pltpu.SemaphoreType.DMA
    V = pltpu.VMEM
    return pl.pallas_call(
        functools.partial(kernel, groups, parts, heads_dev, head_dim, chunk_in, chunk_out),
        out_shape=jax.ShapeDtypeStruct((steps, row_dev, width // parts), BF),
        in_specs=[anywhere] * 14,
        out_specs=vm,
        scratch_shapes=[
            V((layers, 2 * block, channels), BF),
            V((layers, block, mix_width), BF),
            V((layers, channels, block), BF),
            V((layers, row_dev, channels, state_dim), BF),
            V((layers, taps_count - 1, row_dev, channels), BF),
            V((layers, block), F32),
            V((layers, heads_dev), F32),
            V((layers, heads_dev), F32),
            V((layers, heads_dev), F32),
            V((layers, taps_count, channels), F32),
            V((layers, channels), F32),
            pltpu.SMEM((2, 1), jnp.int32),
            V((groups, steps, row_dev, block), BF),
            V((row_dev, LANES), F32),
            V((groups, row_dev, LANES), F32),
            V((steps, rows, block), F32),
            V((rows, LANES), F32),
            V((layers, steps, row_dev, channels), F32),
            V((n_heads, channels), BF),
            V((steps, 2 * rows, 2 * block), BF),
            V((steps, 2 * rows, block), F32),
            V((layers, steps, row_dev, channels), F32),
            V((layers, steps, row_dev, channels), F32),
            V((layers, steps, row_dev, channels), F32),
            V((layers, steps, row_dev, state_dim), F32),
            V((row_dev, channels), F32),
            V((layers, steps, 2, half, row_dev, mix_width + LANES), BF),
            V((layers, steps, half, row_dev, mix_width + LANES), BF),
            V((layers, steps, half, row_dev, mix_width + LANES), BF),
            V((layers, steps, half, row_dev, mix_width + LANES), BF),
            V((layers, steps, n_in, 2, half, pair, chunk_in), BF),
            V((layers, steps, n_in, half, pair, chunk_in), BF),
            V((layers, steps, n_in, half, pair, chunk_in), BF),
            V((layers, steps, n_in, half, pair, chunk_in), BF),
            V((layers, steps, n_in, row_dev, chunk_in), BF),
            V((layers, steps, n_in, groups, row_dev, chunk_in), BF),
            V((layers, steps, n_out, rows, chunk_out), BF),
            V((layers, steps, n_out, parts, rows, chunk_out), BF),
            V((groups, steps, row_dev, block), BF),
            V((share, steps, row_dev, block), BF),
            V((steps, n_out, groups, row_dev, chunk_out), BF),
            V((steps, n_out, share * parts, row_dev, chunk_out), BF),
            V((steps, n_in, rows, chunk_in), F32),
            V((rows, chunk_out), F32),
            V((rows, block), F32),
            dma((layers, 3)),
            dma((layers, n_in)),
            dma((9,)),
            dma,
            dma,
            dma,
            dma,
            dma,
            dma((layers,)),
            dma((layers, steps)),
            dma((layers,)),
            dma((layers, steps)),
            dma((layers,)),
            dma((layers, steps, n_in)),
            dma((layers,)),
            dma((layers, steps, n_in)),
            dma((layers,)),
            dma((layers, steps, n_in)),
            dma((layers,)),
            dma((layers, steps, n_out)),
            dma,
            dma,
            dma,
            dma((steps, n_out)),
        ],
        compiler_params=pltpu.CompilerParams(
            collective_id=0, has_side_effects=True, vmem_limit_bytes=60 * 2**20
        ),
    )(
        embeds, conv, norm_gain, dt_bias, a_log, skip_gain, conv_weight, conv_bias, leave_row, arrive_from,
        state, in_weight, group_weight, out_weight,
    )


def solution(mesh):
    placed = (
        P(None, "grp", None),
        P(None, "grp", "tp", None, None),
        P(None, "grp", None, "tp"),
        P(),
        P(None, "grp", None, "tp"),
        P(None, "grp", None),
        P(None, "tp"),
        P(None, "tp"),
        P(None, "tp"),
        P(None, None, "tp"),
        P(None, "tp"),
        P(None, "tp", "grp"),
        P("grp"),
        P("grp"),
    )
    return jax.shard_map(
        local, mesh=mesh, in_specs=placed, out_specs=P(None, "grp", "tp"), check_vma=False
    )
```

```python
import functools

import jax
import jax.numpy as jnp
from jax import lax
from jax.experimental import pallas as pl
from jax.experimental.pallas import tpu as pltpu
from jax.sharding import PartitionSpec as P

F32 = jnp.float32
BF = jnp.bfloat16
LANES = 128


def iota(shape, dim):
    return lax.broadcasted_iota(jnp.int32, shape, dim)


def mm(a, b):
    return jnp.dot(a, b, preferred_element_type=F32)


def silu(v):
    return v / (1.0 + jnp.exp(-v))


def one_hot(cond):
    return cond.astype(F32).astype(BF)


def remote(src, dst, send_sem, recv_sem, device):
    return pltpu.make_async_remote_copy(
        src_ref=src,
        dst_ref=dst,
        send_sem=send_sem,
        recv_sem=recv_sem,
        device_id=device,
        device_id_type=pl.DeviceIdType.MESH,
    )


def far_first(me, n):
    upper = (2 * me) // n
    order = []
    for k in range(n - 1):
        down = n - 1 - k
        down = down - (me - down + n) // n
        up = k + (k - me + n) // n
        order.append(down + upper * (up - down))
    return order


def exact_mm(values, hot):
    rest = values
    total = jnp.zeros((values.shape[0], hot.shape[1]), F32)
    for _ in range(3):
        piece = rest.astype(BF)
        rest = rest - piece.astype(F32)
        total = total + mm(piece, hot)
    return total


def kernel(
    groups, parts, heads_dev, head_dim, chunk_in, chunk_out,
    emb, conv, gain, dt_bias, a_log, skip, taps, cbias, leave, arrive, state, w_in, w_grp, w_out,
    out,
    win_v, wg_v, wout_v, st_v,
    conv_v, gain_v, bias_v, rate_v, skip_v, taps_v, cbias_v, who,
    emb_r, info, info_r, e32, info32, pre, sel, lhs, hxs, keep_d, keep_u, keep_x, keep_b, y_v,
    m_send, m_pair, m_z, m_recv, a_send, a_pair, a_z, a_recv,
    b_send, b_recv, c_send, c_recv, h_send, h_recv, p_send, p_recv, gat, gat_p, gat_h,
    load_sem, in_sem, small_sem, own_sem, es_sem, er_sem, is_sem, ir_sem, mps_sem, mpr_sem, ms_sem, mr_sem,
    aps_sem, apr_sem, as_sem, ar_sem,
    bs_sem, br_sem, cs_sem, cr_sem, hs_sem, hr_sem, ps_sem, pr_sem,
):
    g = lax.axis_index("grp")
    t = lax.axis_index("tp")
    steps, row_dev, width = emb.shape
    layers = gain.shape[0]
    block = width // groups
    rows = groups * row_dev
    pair = 2 * row_dev
    channels = taps.shape[2]
    taps_count = taps.shape[1]
    state_dim = st_v.shape[3]
    mix_width = wg_v.shape[2]
    n_in = channels // chunk_in
    n_out = block // chunk_out
    share = groups // parts
    half = groups // 2
    core = lax.rem(g, 2)
    chip = g // 2
    partner = g + 1 - 2 * core
    owner = g // share
    w_pairs = w_in.reshape(layers, 2 * block, channels)

    barrier = pltpu.get_barrier_semaphore()
    for d in range(1, groups):
        pl.semaphore_signal(
            barrier, inc=1, device_id={"grp": lax.rem(g + d, groups)},
            device_id_type=pl.DeviceIdType.MESH,
        )
    for d in range(1, parts):
        pl.semaphore_signal(
            barrier, inc=1, device_id={"tp": lax.rem(t + d, parts)},
            device_id_type=pl.DeviceIdType.MESH,
        )

    def arrived(ref, sem):
        remote(ref, ref, sem, sem, {"grp": partner}).wait_recv()

    def left(ref, sem):
        remote(ref, ref, sem, sem, {"grp": partner}).wait_send()

    far_chips = far_first(chip, half)
    far_peers = [2 * to + c for to in far_chips for c in range(2)] + [partner]

    def columns(who_):
        return pl.ds(pl.multiple_of(who_ * block, block), block)

    loads = {}

    def load(name, src, dst, sem):
        loads[name] = pltpu.make_async_copy(src, dst, sem)
        loads[name].start()

    load("leave", leave, who.at[0], small_sem.at[0])
    load("arrive", arrive, who.at[1], small_sem.at[1])
    load("emb", emb.at[:, :, columns(g)], emb_r.at[g], own_sem)
    load("gain", gain.at[:, columns(g)], gain_v, small_sem.at[2])
    load("bias", dt_bias, bias_v, small_sem.at[3])
    load("rate", a_log, rate_v, small_sem.at[4])
    load("skip", skip, skip_v, small_sem.at[5])
    load("taps", taps, taps_v, small_sem.at[6])
    load("cbias", cbias, cbias_v, small_sem.at[7])
    load("conv", conv, conv_v, small_sem.at[8])

    def load_in(l):
        load((l, "grp"), w_grp.at[l], wg_v.at[l], load_sem.at[l, 0])
        for c in range(n_in):
            cols = slice(c * chunk_in, (c + 1) * chunk_in)
            load((l, c), w_pairs.at[l, :, cols], win_v.at[l, :, cols], in_sem.at[l, c])

    def load_rest(l):
        load((l, "state"), state.at[l], st_v.at[l], load_sem.at[l, 1])
        load((l, "out"), w_out.at[l], wout_v.at[l], load_sem.at[l, 2])

    load_in(0)
    loads["leave"].wait()
    loads["arrive"].wait()
    first_half = iota((row_dev, LANES), 1) < LANES // 2
    info[...] = jnp.where(first_half, who[0, 0].astype(F32), who[1, 0].astype(F32))

    pl.semaphore_wait(barrier, groups - 1 + parts - 1)

    for peer in far_peers:
        remote(emb.at[:, :, columns(peer)], emb_r.at[g], es_sem, er_sem, {"grp": peer}).start()
        remote(info, info_r.at[g], is_sem, ir_sem, {"grp": peer}).start()
    info_r[g] = info[...]
    load_rest(0)
    for l in range(1, layers):
        load_in(l)
        load_rest(l)

    n_heads = sel.shape[0]
    sel[...] = one_hot(
        iota((n_heads, channels), 0) == t * heads_dev + iota((n_heads, channels), 1) // head_dim
    )
    own_head = one_hot(iota((heads_dev, channels), 1) // head_dim == iota((heads_dev, channels), 0))
    place = one_hot(iota((heads_dev, n_heads), 1) == t * heads_dev + iota((heads_dev, n_heads), 0))
    spread = one_hot(iota((LANES, 2 * LANES), 1) // 2 == iota((LANES, 2 * LANES), 0))
    own_half = lax.rem(iota((2 * rows, 2 * LANES), 1), 2) == lax.rem(
        iota((2 * rows, 2 * LANES), 0) // row_dev, 2
    )
    dup_row = iota((2 * rows, rows), 0)
    dup = one_hot(iota((2 * rows, rows), 1) == (dup_row // pair) * row_dev + lax.rem(dup_row, row_dev))
    und_col = iota((rows, 2 * rows), 1)
    und_row = iota((rows, 2 * rows), 0)
    undup = one_hot(und_col == (und_row // row_dev) * pair + lax.rem(und_row, row_dev))
    for name in ("bias", "rate", "skip", "cbias", "conv", "taps"):
        loads[name].wait()
    bias_all = exact_mm(bias_v[...], place)
    rate_all = exact_mm(jnp.exp(rate_v[...]), place)
    skip_all = exact_mm(skip_v[...], own_head)
    for l in range(layers):
        for s in range(steps):
            total = jnp.zeros((row_dev, channels), F32)
            for k in range(taps_count - 1):
                if s + k <= taps_count - 2:
                    total = total + conv_v[l, s + k].astype(F32) * taps_v[l, k : k + 1, :]
            pre[l, s] = total + cbias_v[l : l + 1, :]

    loads["gain"].wait()
    loads["emb"].wait()
    arrived(info_r.at[0 : groups - 1], ir_sem)
    arrived(emb_r.at[0 : groups - 1], er_sem)
    for i in range(groups):
        for s in range(steps):
            e32[s, i * row_dev : (i + 1) * row_dev, :] = emb_r[i, s].astype(F32)
        info32[i * row_dev : (i + 1) * row_dev, :] = info_r[i]

    square_shape = (rows, rows)
    row_i = iota(square_shape, 0)
    col_i = iota(square_shape, 1)
    on_diag = row_i == col_i
    leave_of_row = jnp.broadcast_to(info32[:, 0:1], square_shape)
    from_of_row = jnp.broadcast_to(info32[:, LANES // 2 : LANES // 2 + 1], square_shape)
    leave_of_col = jnp.sum(jnp.where(on_diag, leave_of_row, 0.0), axis=0, keepdims=True)
    from_of_col = jnp.sum(jnp.where(on_diag, from_of_row, 0.0), axis=0, keepdims=True)
    slot_row = lax.rem(row_i, row_dev).astype(F32)
    slot_col = lax.rem(col_i, row_dev).astype(F32)
    group_row = (row_i // row_dev).astype(F32)
    group_col = (col_i // row_dev).astype(F32)
    diag = jnp.where(on_diag, 1.0, 0.0)
    hit = jnp.where(group_col == from_of_row, 1.0, 0.0) * jnp.where(slot_col == leave_of_col, 1.0, 0.0)
    to_slot = jnp.where(slot_row == leave_of_row, hit, diag).astype(BF)
    hit_t = jnp.where(group_row == from_of_col, 1.0, 0.0) * jnp.where(slot_row == leave_of_row, 1.0, 0.0)
    to_home = jnp.where(slot_col == leave_of_col, hit_t, diag).astype(BF)

    for s in range(steps):
        start = e32[s].astype(BF)
        for _ in range(s):
            start = mm(to_home, start).astype(BF)
        hxs[s] = mm(dup, start)

    sends = [(info_r.at[0 : groups - 1], is_sem), (emb_r.at[0 : groups - 1], es_sem)]
    slot8 = lax.rem(iota((pair, channels), 0), row_dev)
    waiting = []

    def pass_on():
        l, s, c = waiting.pop(0)
        if c < 0:
            arrived(m_pair.at[l, s], mpr_sem.at[l, s])
            m_z[l, s] = (m_send[l, s, core].astype(F32) + m_pair[l, s].astype(F32)).astype(BF)
            for to in far_chips:
                remote(
                    m_z.at[l, s, to], m_recv.at[l, s, chip], ms_sem.at[l], mr_sem.at[l, s], {"grp": 2 * to + core}
                ).start()
            m_recv[l, s, chip] = m_z[l, s, chip]
        else:
            arrived(a_pair.at[l, s, c], apr_sem.at[l, s, c])
            a_z[l, s, c] = (a_send[l, s, c, core].astype(F32) + a_pair[l, s, c].astype(F32)).astype(BF)
            for to in far_chips:
                remote(
                    a_z.at[l, s, c, to], a_recv.at[l, s, c, chip], as_sem.at[l], ar_sem.at[l, s, c],
                    {"grp": 2 * to + core},
                ).start()
            a_recv[l, s, c, chip] = a_z[l, s, c, chip]

    def enter(l, s):
        hx = hxs[s]
        gained = (hx * gain_v[l : l + 1, :]).astype(BF)
        if s == 0:
            loads[l, "grp"].wait()
        mix = mm(gained, wg_v[l])
        square = jnp.broadcast_to(jnp.sum(hx * hx, axis=1, keepdims=True), (2 * rows, LANES))
        for i in range(groups):
            m_send[l, s, i % 2, i // 2, :, :mix_width] = mix[i * pair : i * pair + row_dev].astype(BF)
            m_send[l, s, i % 2, i // 2, :, mix_width:] = square[i * pair : i * pair + row_dev].astype(BF)
        remote(
            m_send.at[l, s, 1 - core], m_pair.at[l, s], mps_sem.at[l], mpr_sem.at[l, s], {"grp": partner}
        ).start()
        waiting.append((l, s, -1))
        while len(waiting) > 1:
            pass_on()
        for j in range(block // LANES):
            wide = mm(gained[:, j * LANES : (j + 1) * LANES], spread)
            lhs[s, :, 2 * j * LANES : 2 * (j + 1) * LANES] = jnp.where(own_half, wide, 0.0).astype(BF)
        for c in range(n_in):
            if s == 0:
                loads[l, c].wait()
            acc = mm(lhs[s], win_v[l, :, c * chunk_in : (c + 1) * chunk_in])
            for i in range(groups):
                a_send[l, s, c, i % 2, i // 2] = acc[i * pair : (i + 1) * pair].astype(BF)
            remote(
                a_send.at[l, s, c, 1 - core], a_pair.at[l, s, c], aps_sem.at[l], apr_sem.at[l, s, c], {"grp": partner}
            ).start()
            waiting.append((l, s, c))
            while len(waiting) > 1:
                pass_on()
        if s == steps - 1:
            pass_on()

    def mixer(l, s):
        arrived(m_recv.at[l, s, 0 : half - 1], mr_sem.at[l, s])
        msum = m_recv[l, s, 0].astype(F32)
        for i in range(1, half):
            msum = msum + m_recv[l, s, i].astype(F32)
        scale = lax.rsqrt(msum[:, mix_width : mix_width + 1] / width + 1e-05)
        b_mat = msum[:, :state_dim] * scale
        c_mat = msum[:, state_dim : 2 * state_dim] * scale
        keep_b[l, s] = b_mat
        pre_dt = msum[:, 2 * state_dim : mix_width] * scale + bias_all[l : l + 1, :]
        step_size = jnp.maximum(pre_dt, 0.0) + jnp.log1p(jnp.exp(-jnp.abs(pre_dt)))
        decay = jnp.exp(-step_size * rate_all[l : l + 1, :])
        pieces = []
        for v in (step_size, decay):
            hi = v.astype(BF).astype(F32)
            pieces += [hi, v - hi]
        wide = mm(jnp.concatenate(pieces, axis=0).astype(BF), sel[...])
        step_ch = wide[0:row_dev] + wide[row_dev:pair]
        keep_d[l, s] = wide[pair : pair + row_dev] + wide[pair + row_dev : 2 * pair]
        bc = [jnp.sum(keep_b[l, e] * c_mat, axis=1, keepdims=True) for e in range(s + 1)]
        c_hi = c_mat.astype(BF).astype(F32)
        c_both = jnp.concatenate([c_hi, c_mat - c_hi], axis=0).astype(BF)
        if s == 0:
            loads[l, "state"].wait()
        total = jnp.zeros((pair, channels), F32)
        for r in range(row_dev):
            got = lax.dot_general(
                c_both, st_v[l, r], (((1,), (1,)), ((), ())), preferred_element_type=F32
            )
            total = jnp.where(slot8 == r, got, total)
        y_v[...] = total[0:row_dev] + total[row_dev:pair]

        for c in range(n_in):
            cols = slice(c * chunk_in, (c + 1) * chunk_in)
            arrived(a_recv.at[l, s, c, 0 : half - 1], ar_sem.at[l, s, c])
            asum = a_recv[l, s, c, 0].astype(F32)
            for i in range(1, half):
                asum = asum + a_recv[l, s, c, i].astype(F32)
            x = (asum[0:row_dev] * scale).astype(BF).astype(F32)
            z = asum[row_dev:pair] * scale
            keep_x[l, s, :, cols] = x
            conv_sum = pre[l, s, :, cols] + x * taps_v[l, taps_count - 1 : taps_count, cols]
            for e in range(s):
                tap = taps_count - 1 + e - s
                if tap >= 0:
                    conv_sum = conv_sum + keep_x[l, e, :, cols] * taps_v[l, tap : tap + 1, cols]
            xc = silu(conv_sum)
            keep_u[l, s, :, cols] = step_ch[:, cols] * xc
            acc_y = y_v[:, cols]
            for e in range(s + 1):
                acc_y = keep_d[l, e, :, cols] * acc_y + keep_u[l, e, :, cols] * bc[e]
            gated = ((acc_y + skip_all[l : l + 1, cols] * xc) * silu(z)).astype(BF)
            b_send[l, s, c] = gated
            b_recv[l, s, c, g] = gated
            for peer in far_peers:
                remote(
                    b_send.at[l, s, c], b_recv.at[l, s, c, g], bs_sem.at[l], br_sem.at[l, s, c], {"grp": peer}
                ).start()

    def project(l, s):
        if s == 0:
            loads[l, "out"].wait()
        gated_all = []
        for c in range(n_in):
            arrived(b_recv.at[l, s, c, 0 : groups - 1], br_sem.at[l, s, c])
            for i in range(groups):
                gat[s, c, i * row_dev : (i + 1) * row_dev, :] = b_recv[l, s, c, i].astype(F32)
            part = gat[s, c].astype(BF)
            if l == layers - 1:
                for _ in range(s):
                    part = mm(to_slot, part).astype(BF)
            gated_all.append(part)
        gated_all = jnp.concatenate(gated_all, axis=1)
        for n in range(n_out):
            part = mm(gated_all, wout_v[l, :, n * chunk_out : (n + 1) * chunk_out])
            if l < layers - 1:
                c_send[l, s, n] = part.astype(BF)
                c_recv[l, s, n, t] = c_send[l, s, n]
                for d in range(parts - 1, 0, -1):
                    remote(
                        c_send.at[l, s, n], c_recv.at[l, s, n, t], cs_sem.at[l], cr_sem.at[l, s, n],
                        {"tp": lax.rem(t + d, parts)},
                    ).start()
            else:
                spot = lax.rem(g, share) * parts + t
                gat_p[...] = part
                for i in range(groups):
                    p_send[s, n, i] = gat_p[i * row_dev : (i + 1) * row_dev, :].astype(BF)
                for peer in far_peers:
                    remote(
                        p_send.at[s, n, peer], p_recv.at[s, n, spot], ps_sem, pr_sem.at[s, n],
                        {"grp": peer, "tp": owner},
                    ).start()

                @pl.when(owner == t)
                def _():
                    p_recv[s, n, spot] = p_send[s, n, g]

                @pl.when(owner != t)
                def _():
                    remote(
                        p_send.at[s, n, g], p_recv.at[s, n, spot], ps_sem, pr_sem.at[s, n],
                        {"grp": g, "tp": owner},
                    ).start()

    def update(l, s):
        for n in range(n_out):
            arrived(c_recv.at[l, s, n, 0 : parts - 1], cr_sem.at[l, s, n])
            dsum = c_recv[l, s, n, 0].astype(F32)
            for i in range(1, parts):
                dsum = dsum + c_recv[l, s, n, i].astype(F32)
            cols = slice(n * chunk_out, (n + 1) * chunk_out)
            hxs[s, :, cols] = (hxs[s, :, cols] + mm(dup, dsum.astype(BF))).astype(BF).astype(F32)

    for l in range(layers):
        for s in range(steps):
            if l > 0:
                update(l - 1, s)
            enter(l, s)
        if l == layers - 1:
            for s in range(steps):
                final = mm(undup, hxs[s].astype(BF))
                for _ in range(s):
                    final = mm(to_slot, final.astype(BF))
                gat_h[...] = final
                for i in range(groups):
                    h_send[i, s] = gat_h[i * row_dev : (i + 1) * row_dev, :].astype(BF)

            @pl.when(owner == t)
            def _():
                for peer in far_peers:
                    remote(
                        h_send.at[peer], h_recv.at[lax.rem(g, share)], hs_sem, hr_sem, {"grp": peer}
                    ).start()
                h_recv[lax.rem(g, share)] = h_send[g]

        for ref, sem in sends:
            left(ref, sem)
        for s in range(steps):
            mixer(l, s)
        for s in range(steps):
            project(l, s)
        sends = [
            (m_pair.at[l], mps_sem.at[l]),
            (a_pair.at[l], aps_sem.at[l]),
            (m_recv.at[l, :, 0 : half - 1], ms_sem.at[l]),
            (a_recv.at[l, :, :, 0 : half - 1], as_sem.at[l]),
            (b_recv.at[l, :, :, 0 : groups - 1], bs_sem.at[l]),
        ]
        if l < layers - 1:
            sends.append((c_recv.at[l, :, :, 0 : parts - 1], cs_sem.at[l]))

    for ref, sem in sends:
        left(ref, sem)

    @pl.when(owner == t)
    def _():
        left(h_send.at[0 : groups - 1], hs_sem)
        left(p_send.at[:, :, 0 : groups - 1], ps_sem)
        if share > 1:
            arrived(h_recv.at[0 : share - 1], hr_sem)

    @pl.when(owner != t)
    def _():
        left(p_send, ps_sem)
        arrived(h_recv, hr_sem)

    for s in range(steps):
        for n in range(n_out):

            @pl.when(owner == t)
            def _():
                arrived(p_recv.at[s, n, 0 : share * parts - 1], pr_sem.at[s, n])

            @pl.when(owner != t)
            def _():
                arrived(p_recv.at[s, n], pr_sem.at[s, n])

            for j in range(share):
                dsum = p_recv[s, n, j * parts].astype(F32)
                for i in range(1, parts):
                    dsum = dsum + p_recv[s, n, j * parts + i].astype(F32)
                result = h_recv[j, s, :, n * chunk_out : (n + 1) * chunk_out].astype(F32) + dsum.astype(BF).astype(F32)
                out[s, :, j * block + n * chunk_out : j * block + (n + 1) * chunk_out] = result.astype(BF)


def local(
    embeds, ssm_state, conv_state, norm_gain, in_weight, group_weight, dt_bias, a_log,
    skip_gain, conv_weight, conv_bias, out_weight, leave_row, arrive_from,
):
    groups = lax.axis_size("grp")
    parts = lax.axis_size("tp")
    steps, row_dev, width = embeds.shape
    layers, _, heads_dev, head_dim, state_dim = ssm_state.shape
    block = in_weight.shape[1]
    channels = in_weight.shape[3]
    mix_width = group_weight.shape[2]
    n_heads = mix_width - 2 * state_dim
    taps_count = conv_weight.shape[1]
    rows = groups * row_dev
    pair = 2 * row_dev
    share = groups // parts
    half = groups // 2
    chunk_in = min(1024, channels)
    chunk_out = min(512, block)
    n_in = channels // chunk_in
    n_out = block // chunk_out

    state = ssm_state.reshape(layers, row_dev, channels, state_dim)
    conv = conv_state.transpose(0, 2, 1, 3)
    vm = pl.BlockSpec(memory_space=pltpu.VMEM)
    anywhere = pl.BlockSpec(memory_space=pl.ANY)
    dma = pltpu.SemaphoreType.DMA
    V = pltpu.VMEM
    return pl.pallas_call(
        functools.partial(kernel, groups, parts, heads_dev, head_dim, chunk_in, chunk_out),
        out_shape=jax.ShapeDtypeStruct((steps, row_dev, width // parts), BF),
        in_specs=[anywhere] * 14,
        out_specs=vm,
        scratch_shapes=[
            V((layers, 2 * block, channels), BF),
            V((layers, block, mix_width), BF),
            V((layers, channels, block), BF),
            V((layers, row_dev, channels, state_dim), BF),
            V((layers, taps_count - 1, row_dev, channels), BF),
            V((layers, block), F32),
            V((layers, heads_dev), F32),
            V((layers, heads_dev), F32),
            V((layers, heads_dev), F32),
            V((layers, taps_count, channels), F32),
            V((layers, channels), F32),
            pltpu.SMEM((2, 1), jnp.int32),
            V((groups, steps, row_dev, block), BF),
            V((row_dev, LANES), F32),
            V((groups, row_dev, LANES), F32),
            V((steps, rows, block), F32),
            V((rows, LANES), F32),
            V((layers, steps, row_dev, channels), F32),
            V((n_heads, channels), BF),
            V((steps, 2 * rows, 2 * block), BF),
            V((steps, 2 * rows, block), F32),
            V((layers, steps, row_dev, channels), F32),
            V((layers, steps, row_dev, channels), F32),
            V((layers, steps, row_dev, channels), F32),
            V((layers, steps, row_dev, state_dim), F32),
            V((row_dev, channels), F32),
            V((layers, steps, 2, half, row_dev, mix_width + LANES), BF),
            V((layers, steps, half, row_dev, mix_width + LANES), BF),
            V((layers, steps, half, row_dev, mix_width + LANES), BF),
            V((layers, steps, half, row_dev, mix_width + LANES), BF),
            V((layers, steps, n_in, 2, half, pair, chunk_in), BF),
            V((layers, steps, n_in, half, pair, chunk_in), BF),
            V((layers, steps, n_in, half, pair, chunk_in), BF),
            V((layers, steps, n_in, half, pair, chunk_in), BF),
            V((layers, steps, n_in, row_dev, chunk_in), BF),
            V((layers, steps, n_in, groups, row_dev, chunk_in), BF),
            V((layers, steps, n_out, rows, chunk_out), BF),
            V((layers, steps, n_out, parts, rows, chunk_out), BF),
            V((groups, steps, row_dev, block), BF),
            V((share, steps, row_dev, block), BF),
            V((steps, n_out, groups, row_dev, chunk_out), BF),
            V((steps, n_out, share * parts, row_dev, chunk_out), BF),
            V((steps, n_in, rows, chunk_in), F32),
            V((rows, chunk_out), F32),
            V((rows, block), F32),
            dma((layers, 3)),
            dma((layers, n_in)),
            dma((9,)),
            dma,
            dma,
            dma,
            dma,
            dma,
            dma((layers,)),
            dma((layers, steps)),
            dma((layers,)),
            dma((layers, steps)),
            dma((layers,)),
            dma((layers, steps, n_in)),
            dma((layers,)),
            dma((layers, steps, n_in)),
            dma((layers,)),
            dma((layers, steps, n_in)),
            dma((layers,)),
            dma((layers, steps, n_out)),
            dma,
            dma,
            dma,
            dma((steps, n_out)),
        ],
        compiler_params=pltpu.CompilerParams(
            collective_id=0, has_side_effects=True, vmem_limit_bytes=60 * 2**20
        ),
    )(
        embeds, conv, norm_gain, dt_bias, a_log, skip_gain, conv_weight, conv_bias, leave_row, arrive_from,
        state, in_weight, group_weight, out_weight,
    )


def solution(mesh):
    placed = (
        P(None, "grp", None),
        P(None, "grp", "tp", None, None),
        P(None, "grp", None, "tp"),
        P(),
        P(None, "grp", None, "tp"),
        P(None, "grp", None),
        P(None, "tp"),
        P(None, "tp"),
        P(None, "tp"),
        P(None, None, "tp"),
        P(None, "tp"),
        P(None, "tp", "grp"),
        P("grp"),
        P("grp"),
    )
    return jax.shard_map(
        local, mesh=mesh, in_specs=placed, out_specs=P(None, "grp", "tp"), check_vma=False
    )
```
